256 devices in a mesh: px: 4 (over z_lo), py: 8 (over y, core), ch: 8 (over z_hi, x).
Axes of the slice: x: 4, y: 4, z: 8 (z_hi: 2, z_lo: 4; z = z_hi * 4 + z_lo), core: 2. Of those that a mesh axis runs over, the one named last changes fastest.
Arguments:
- features: bfloat16 [128, 12, 8, 4, 512], P('ch', None, 'py', 'px'), may hold values from -6 to 6
- cotangent: bfloat16 [128, 12, 8, 4, 512], P('ch', None, 'py', 'px'), may hold values from -6 to 6
- weight: bfloat16 [3, 3, 128, 128], replicated, may hold values from -0.1875 to 0.1875
- edge_table: int32 [12, 4, 3], replicated, may hold values from 0 to 11, as said below
- corner_table: int32 [12, 4, 2], replicated, may hold values from 0 to 11, as said below
Outputs:
- activation: bfloat16 [128, 12, 8, 4, 512], P('ch', None, 'py', 'px')
- input_grad: bfloat16 [128, 12, 8, 4, 512], P('ch', None, 'py', 'px')
The draws below stay inside these ranges and needn't reach their ends.
Inputs may be any that keep to these rules, and one draw needn't show every extreme that they name: edge_table[f, e] = (g, s, r): beyond edge e of face f lie the pixels of side s of face g, in reverse order if r = 1; every side of every face is named exactly once, and if (f, e) names (g, s) then (g, s) names (f, e) with the same r. corner_table[f, c] = (h, q): corner c of face f takes corner pixel q of face h; in each corner column every face appears once, and each q appears 12 times.
All inputs are finite; a program needn't handle non-finite values.
Results may differ from the reference program's by a relative error of at most 0.0049.
Values may be sent and summed in bfloat16 or wider, within the bound.
A program may use at most 192 MiB of HBM per device.

```python
import jax
import jax.numpy as jnp
from jax import lax

C = 128
FACES = 12
RB = 32
RA = 16
TILE = 512
N_PX = 4
N_PY = 8


def draw_edge_table(key, part):
    order = jax.random.permutation(jax.random.fold_in(key, 11), FACES * 4)
    firsts = order[0::2]
    seconds = order[1::2]
    partner = jnp.zeros((FACES * 4,), jnp.int32).at[firsts].set(seconds).at[seconds].set(firsts)
    pair_flip = jax.random.randint(jax.random.fold_in(key, 12), (FACES * 2,), 0, 2)
    flips = jnp.zeros((FACES * 4,), jnp.int32).at[firsts].set(pair_flip).at[seconds].set(pair_flip)
    table = jnp.stack([partner // 4, partner % 4, flips], axis=1).reshape(FACES, 4, 3)
    return table.astype(jnp.int32)


def draw_corner_table(key, part):
    sources = jnp.stack([jax.random.permutation(jax.random.fold_in(key, 20 + corner_num), FACES) for corner_num in range(4)], axis=1)
    pixels = (jax.random.permutation(jax.random.fold_in(key, 30), FACES * 4) % 4).reshape(FACES, 4)
    return jnp.stack([sources, pixels], axis=2).astype(jnp.int32)


def levels(stream_key, shape, pieces, smallest, high):
    gain, own = 1.0, jax.random.fold_in(stream_key, 6)
    for dim, blocks in pieces:
        draws = jnp.exp(jax.random.uniform(jax.random.fold_in(own, dim), (blocks,), jnp.float32, smallest / len(pieces), high / len(pieces)))
        gain = gain * jnp.repeat(draws, shape[dim] // blocks).reshape([-1 if axis == dim else 1 for axis in range(len(shape))])
    return gain


def bell_draw(own_key, extent, deviation, bound, pieces=(), held_as=jnp.bfloat16):
    gain = levels(own_key, extent, pieces, -0.22, 0.18) if pieces else 1.0
    array = jax.random.normal(own_key, extent, jnp.float32) * deviation * gain
    return jnp.minimum(jnp.maximum(array, -bound), bound).astype(held_as)


def setup_inputs(seed: int = 0) -> dict:
    key_of = jax.random.split(jax.random.key(seed), 6)
    return {
        "features": bell_draw(key_of[0], (C, FACES, N_PY, N_PX, TILE), 1.0, 6.0, ((0, 8), (2, 8), (3, 4))),
        "cotangent": bell_draw(key_of[1], (C, FACES, N_PY, N_PX, TILE), 1.0, 6.0, ((0, 8), (2, 8), (3, 4))),
        "weight": bell_draw(key_of[2], (3, 3, C, C), (9 * C) ** -0.5, 0.1875),
        "edge_table": draw_edge_table(jax.random.fold_in(key_of[5], 71), 0),
        "corner_table": draw_corner_table(jax.random.fold_in(key_of[5], 71), 0),
    }


def to_grid(blocked):
    chan_count = blocked.shape[0]
    face_count = blocked.shape[1]
    tiles_col = blocked.shape[2]
    tiles_row = blocked.shape[3]
    shaped = blocked.reshape(chan_count, face_count, tiles_col, tiles_row, RA, RB)
    shaped = jnp.transpose(shaped, (0, 1, 2, 4, 3, 5))
    return shaped.reshape(chan_count, face_count, tiles_col * RA, tiles_row * RB)


def to_blocked(grid):
    chan_count = grid.shape[0]
    face_count = grid.shape[1]
    tiles_col = grid.shape[2] // RA
    tiles_row = grid.shape[3] // RB
    shaped = grid.reshape(chan_count, face_count, tiles_col, RA, tiles_row, RB)
    shaped = jnp.transpose(shaped, (0, 1, 2, 4, 3, 5))
    return shaped.reshape(chan_count, face_count, tiles_col, tiles_row, RA * RB)


def edge_strips(lines, edge_table, corner_table):
    chan_count = lines.shape[0]
    face_count = lines.shape[1]
    side_len = lines.shape[3]
    flat_lines = lines.reshape(chan_count, face_count * 4, side_len)
    pixels = jnp.stack([lines[:, :, 0, 0], lines[:, :, 0, -1], lines[:, :, 1, 0], lines[:, :, 1, -1]], axis=2).reshape(chan_count, face_count * 4)
    corner_index = (corner_table[:, :, 0] * 4 + corner_table[:, :, 1]).astype(jnp.int32)
    corner_vals = jnp.take(pixels, corner_index, axis=1)
    strips = []
    for edge_num, start_corner, end_corner in ((0, 0, 1), (1, 2, 3), (2, 0, 2), (3, 1, 3)):
        source_row = (edge_table[:, edge_num, 0] * 4 + edge_table[:, edge_num, 1]).astype(jnp.int32)
        strip_line = jnp.take(flat_lines, source_row, axis=1)
        flipped = (edge_table[:, edge_num, 2] == 1)[None, :, None]
        strip_line = jnp.where(flipped, strip_line[:, :, ::-1], strip_line)
        strips.append(jnp.concatenate([corner_vals[:, :, start_corner:start_corner + 1], strip_line, corner_vals[:, :, end_corner:end_corner + 1]], axis=2))
    return strips


def pad_whole(field, edge_table, corner_table):
    lines = jnp.stack([field[:, :, 0, :], field[:, :, -1, :], field[:, :, :, 0], field[:, :, :, -1]], axis=2)
    strips = edge_strips(lines, edge_table, corner_table)
    padded = jnp.pad(field, ((0, 0), (0, 0), (1, 1), (1, 1)))
    padded = padded.at[:, :, 0, :].set(strips[0])
    padded = padded.at[:, :, -1, :].set(strips[1])
    padded = padded.at[:, :, :, 0].set(strips[2])
    padded = padded.at[:, :, :, -1].set(strips[3])
    return padded


def gate_outputs(preact, cotangent):
    sigmoid_val = jax.nn.sigmoid(preact)
    activation = (preact * sigmoid_val).astype(jnp.bfloat16)
    gated = (cotangent.astype(jnp.float32) * sigmoid_val * (1.0 + preact * (1.0 - sigmoid_val))).astype(jnp.bfloat16)
    return activation, gated


def reference(features, cotangent, weight, edge_table, corner_table):
    taps = weight.astype(jnp.float32)
    features = to_grid(features)
    cotangent = to_grid(cotangent)
    side_len = features.shape[2]
    feat_pad = pad_whole(features, edge_table, corner_table)

    def forward_face(operands):
        face_pad, face_cot = operands
        summed = jnp.zeros((taps.shape[2], side_len, side_len), jnp.float32)
        for tap_row in range(3):
            for tap_col in range(3):
                window = face_pad[:, tap_row:tap_row + side_len, tap_col:tap_col + side_len].astype(jnp.float32)
                summed = summed + jnp.einsum("oc,cab->oab", taps[tap_row, tap_col], window, precision=lax.Precision.HIGHEST)
        return gate_outputs(summed, face_cot)

    act_faces, gated_faces = lax.map(forward_face, (jnp.moveaxis(feat_pad, 1, 0), jnp.moveaxis(cotangent, 1, 0)))
    activation = jnp.moveaxis(act_faces, 0, 1)
    gated = jnp.moveaxis(gated_faces, 0, 1)
    grad_pad = pad_whole(gated, edge_table, corner_table)

    def backward_face(face_pad):
        summed = jnp.zeros((taps.shape[3], side_len, side_len), jnp.float32)
        for tap_row in range(3):
            for tap_col in range(3):
                window = face_pad[:, 2 - tap_row:2 - tap_row + side_len, 2 - tap_col:2 - tap_col + side_len].astype(jnp.float32)
                summed = summed + jnp.einsum("oc,oab->cab", taps[tap_row, tap_col], window, precision=lax.Precision.HIGHEST)
        return summed.astype(jnp.bfloat16)

    grad_faces = lax.map(backward_face, jnp.moveaxis(grad_pad, 1, 0))
    input_grad = jnp.moveaxis(grad_faces, 0, 1)
    return to_blocked(activation), to_blocked(input_grad)
```

```python
import functools

import jax
import jax.numpy as jnp
from jax import lax
from jax.experimental import pallas as pl
from jax.experimental.pallas import tpu as pltpu
from jax.sharding import PartitionSpec as P

MESH = pl.DeviceIdType.MESH
F32 = jnp.float32
BF16 = jnp.bfloat16
FACES, CB, RA, RB, TILE = 12, 16, 16, 32, 512
N_PX, N_PY, N_X, N_Z = 4, 8, 4, 2
SIDE = 128
RING = 128
WIDE = TILE + RING

TOP, BOTTOM, LEFT, RIGHT = 0, 34, 68, 84
HALO = (
    (0, 1, 1, 0),
    (0, -1, 0, 1),
    (1, 0, 2, 2),
    (-1, 0, 2, 3),
    (1, 1, 1, 4),
    (-1, 1, 1, 5),
    (1, -1, 0, 6),
    (-1, -1, 0, 7),
)


def iota(shape, dim):
    return lax.broadcasted_iota(jnp.int32, shape, dim)


def ones_where(mask):
    return jnp.where(mask, 1.0, 0.0).astype(BF16)


def dot(a, b):
    return jnp.dot(a, b, preferred_element_type=F32)


def fill_selectors(sbd, sring, sline, scol, sconv):
    p, n = iota((TILE, 128), 0), iota((TILE, 128), 1)
    i = n % 32
    for kind in range(3):
        if kind == 0:
            src = i
        elif kind == 1:
            src = (RA - 1) * RB + i
        else:
            src = jnp.where(i < 16, RB * i, RB * (i - 16) + RB - 1)
        hit = p == src
        for k in range(4):
            sbd[k, :, 128 * kind : 128 * kind + 128] = ones_where(hit & (n // 32 == k))
    row, m = iota((128, 128), 0), iota((128, 128), 1)
    k, i = row // 32, row % 32
    aims = (
        TOP + 1 + i,
        BOTTOM + 1 + i,
        jnp.where(i >= 16, LEFT + i - 16, -1),
        jnp.where(i < 16, RIGHT + i, -1),
        jnp.where(i == 31, TOP, -1),
        jnp.where(i == 0, TOP + 33, -1),
        jnp.where(i == 31, BOTTOM, -1),
        jnp.where(i == 0, BOTTOM + 33, -1),
    )
    for slot, aim in enumerate(aims):
        for face in range(4):
            sring[128 * slot : 128 * slot + 128, 128 * face : 128 * face + 128] = ones_where(
                (k == face) & (m == aim)
            )
    for face in range(4):
        for q in range(N_PX):
            sline[128 * q : 128 * q + 128, 128 * face : 128 * face + 128] = ones_where(
                (k == face) & (m == 32 * q + i)
            )
        for q in range(N_PY):
            for far in range(2):
                part = (i >= 16) if far else (i < 16)
                scol[far, 128 * q : 128 * q + 128, 128 * face : 128 * face + 128] = ones_where(
                    (k == face) & part & (m == 16 * q + i - 16 * far)
                )
    lane, p = iota((128, TILE), 0), iota((128, TILE), 1)
    for tap in range(9):
        pa, pb = p // RB + tap // 3, p % RB + tap % 3
        cell = jnp.where(
            pa == 0,
            TOP + pb,
            jnp.where(
                pa == RA + 1,
                BOTTOM + pb,
                jnp.where(pb == 0, LEFT + pa - 1, jnp.where(pb == RB + 1, RIGHT + pa - 1, -1)),
            ),
        )
        sconv[128 * tap : 128 * tap + 128, :] = ones_where(lane == cell)


def kernel(
    edge_ref,
    corner_ref,
    feat_ref,
    cot_ref,
    w_ref,
    act_ref,
    grad_ref,
    held,
    bd,
    hal,
    lin,
    full,
    ring,
    pre,
    ringy,
    gated,
    wst,
    sbd,
    sring,
    sline,
    scol,
    sconv,
    ag_send,
    ag_recv,
    halo_send,
    halo_recv,
    line_send,
    line_recv,
):
    px, py, ch = lax.axis_index("px"), lax.axis_index("py"), lax.axis_index("ch")
    z, x = ch // N_X, ch % N_X
    up_x = z * N_X + (x + 1) % N_X
    down_x = z * N_X + (x + N_X - 1) % N_X
    far = (1 - z) * N_X + x
    far_up = (1 - z) * N_X + (x + 1) % N_X
    far_down = (1 - z) * N_X + (x + N_X - 1) % N_X

    def on_border(qx, qy):
        return (qx == 0) | (qx == N_PX - 1) | (qy == 0) | (qy == N_PY - 1)

    border = on_border(px, py)
    sides = (py == 0, py == N_PY - 1, px == 0, px == N_PX - 1)

    barrier = pltpu.get_barrier_semaphore()

    def greet(t, carry):
        tx, ty = t // N_PY, t % N_PY

        @pl.when((tx != px) | (ty != py))
        def _():
            pl.semaphore_signal(barrier, inc=1, device_id={"px": tx, "py": ty}, device_id_type=MESH)

        return carry

    lax.fori_loop(0, N_PX * N_PY, greet, 0)
    for peer in (far, up_x, down_x):
        pl.semaphore_signal(barrier, inc=1, device_id={"ch": peer}, device_id_type=MESH)

    fill_selectors(sbd, sring, sline, scol, sconv)
    pick = ones_where(iota((CB, 128), 1) == CB * ch + iota((CB, 128), 0))
    for tap in range(9):
        wst[0, CB * tap : CB * tap + CB, :] = w_ref[tap, pl.ds(pl.multiple_of(CB * ch, CB), CB), :]
        wst[1, CB * tap : CB * tap + CB, :] = lax.dot_general(
            pick, w_ref[8 - tap], (((1,), (1,)), ((), ())), preferred_element_type=F32
        ).astype(BF16)
    for s in range(2):
        for dx, dy, kind, slot in HALO:
            sx, sy = px - dx, py - dy

            @pl.when((sx < 0) | (sx >= N_PX) | (sy < 0) | (sy >= N_PY))
            def _():
                hal[s, slot] = jnp.zeros((3 * CB, 128), BF16)

    pl.semaphore_wait(barrier, N_PX * N_PY - 1 + 3)

    def rows(c):
        return pl.ds(pl.multiple_of(CB * c, CB), CB)

    def ag_copy(s, kind, index):
        block, target, faces = (
            (ch, far, (0, 12)),
            (ch, up_x, (0, 12)),
            (ch, down_x, (0, 12)),
            (far, up_x, (0, 12)),
            (far, down_x, (0, 12)),
            (down_x, up_x, (0, 6)),
            (up_x, down_x, (6, 12)),
            (far_down, up_x, (0, 6)),
            (far_up, down_x, (6, 12)),
        )[index]
        lanes = pl.ds(0, TILE) if kind == 0 else pl.ds(TILE, RING)
        ref = held.at[s, pl.ds(faces[0], faces[1] - faces[0]), rows(block), lanes]
        return pltpu.make_async_remote_copy(
            src_ref=ref,
            dst_ref=ref,
            send_sem=ag_send.at[s, kind, index],
            recv_sem=ag_recv.at[s, kind, index],
            device_id={"ch": target},
            device_id_type=MESH,
        )

    def halo_copy(s, n):
        dx, dy, kind, slot = HALO[n]
        return pltpu.make_async_remote_copy(
            src_ref=bd.at[s, kind],
            dst_ref=hal.at[s, slot],
            send_sem=halo_send.at[s, slot],
            recv_sem=halo_recv.at[s, slot],
            device_id={"px": px + dx, "py": py + dy},
            device_id_type=MESH,
        )

    def inside(qx, qy):
        return (qx >= 0) & (qx < N_PX) & (qy >= 0) & (qy < N_PY)

    my_slots = (px, N_PX + px, 2 * N_PX + py, 2 * N_PX + N_PY + py)

    def line_copy(s, side, t):
        return pltpu.make_async_remote_copy(
            src_ref=bd.at[s, min(side, 2)],
            dst_ref=lin.at[s, my_slots[side]],
            send_sem=line_send.at[s, side, t],
            recv_sem=line_recv.at[s, my_slots[side]],
            device_id={"px": t // N_PY, "py": t % N_PY},
            device_id_type=MESH,
        )

    def each_line_copy(s, act):
        for side in range(4):

            @pl.when(sides[side])
            def _():
                def one(t, carry):
                    tx, ty = t // N_PY, t % N_PY

                    @pl.when(on_border(tx, ty) & ((tx != px) | (ty != py)))
                    def _():
                        act(line_copy(s, side, t))

                    return carry

                lax.fori_loop(0, N_PX * N_PY, one, 0)

    def make_ring(s):
        cells = jnp.concatenate([hal[s, slot] for slot in range(8)], axis=1)
        inner = dot(cells, sring[...])
        for q in range(3):
            for k in range(4):
                ring[4 * q + k] = inner[CB * q : CB * q + CB, 128 * k : 128 * k + 128]

        @pl.when(border)
        def _():
            for side in range(4):
                first, count = ((0, 4), (4, 4), (8, 8), (16, 8))[side]
                parts = jnp.concatenate([lin[s, first + q] for q in range(count)], axis=1)
                table = sline[...] if side < 2 else scol[side - 2]
                lines = dot(parts, table).astype(BF16)
                for q in range(3):
                    for k in range(4):
                        full[12 * side + 4 * q + k] = lines[
                            CB * q : CB * q + CB, 128 * k : 128 * k + 128
                        ]
            t, n = iota((128, 128), 0), iota((128, 128), 1)
            for edge in range(4):

                @pl.when(sides[edge])
                def _():
                    none = jnp.full((128, 128), -1000, jnp.int32)
                    if edge < 2:
                        base = (TOP, BOTTOM)[edge]
                        at = jnp.where(
                            (n >= base) & (n < base + 34), RB * px - 1 + n - base, none
                        )
                    else:
                        base = (LEFT, RIGHT)[edge - 2]
                        shift = 33 * (edge - 2)
                        at = jnp.where((n >= base) & (n < base + 16), RA * py + n - base, none)
                        at = jnp.where(n == TOP + shift, RA * py - 1, at)
                        at = jnp.where(n == BOTTOM + shift, RA * py + RA, at)

                    def face_edge(f, carry):
                        e = 12 * f + 3 * edge
                        line = full[12 * edge_ref[e + 1] + edge_ref[e]]
                        src = jnp.where(edge_ref[e + 2] == 1, SIDE - 1 - at, at)
                        ring[f] += dot(line, ones_where(t == src))
                        return carry

                    lax.fori_loop(0, FACES, face_edge, 0)

            for corner in range(4):
                lane = (TOP, TOP + 33, BOTTOM, BOTTOM + 33)[corner]

                @pl.when(sides[corner // 2] & sides[2 + corner % 2])
                def _():
                    def face_corner(f, carry):
                        c = 8 * f + 2 * corner
                        q = corner_ref[c + 1]
                        line = full[12 * (q // 2) + corner_ref[c]]
                        hit = (t == (SIDE - 1) * (q % 2)) & (n == lane)
                        ring[f] += dot(line, ones_where(hit))
                        return carry

                    lax.fori_loop(0, FACES, face_corner, 0)

        held[s, :, rows(ch), TILE:WIDE] = ring[...].astype(BF16)

    def gather(s, v_ref):
        held[s, :, rows(ch), 0:TILE] = v_ref[...]
        for index in range(3):
            ag_copy(s, 0, index).start()
        packed = None
        for k in range(4):
            part = jnp.concatenate([v_ref[4 * q + k] for q in range(3)], axis=0)
            term = dot(part, sbd[k])
            packed = term if packed is None else packed + term
        packed = packed.astype(BF16)
        for kind in range(3):
            bd[s, kind] = packed[:, 128 * kind : 128 * kind + 128]
        for n, (dx, dy, kind, slot) in enumerate(HALO):

            @pl.when(inside(px + dx, py + dy))
            def _():
                halo_copy(s, n).start()

        for side in range(4):

            @pl.when(sides[side])
            def _():
                lin[s, my_slots[side]] = bd[s, min(side, 2)]

        each_line_copy(s, lambda copy: copy.start())

        for n, (dx, dy, kind, slot) in enumerate(HALO):

            @pl.when(inside(px - dx, py - dy))
            def _():
                halo_copy(s, n).wait_recv()

        @pl.when(border)
        def _():
            def arrived(j, first, qx, qy):
                @pl.when((qx != px) | (qy != py))
                def _():
                    pltpu.make_async_remote_copy(
                        src_ref=bd.at[s, 0],
                        dst_ref=lin.at[s, j],
                        send_sem=line_send.at[s, 0, 0],
                        recv_sem=line_recv.at[s, j],
                        device_id={"px": px, "py": py},
                        device_id_type=MESH,
                    ).wait_recv()

            for q in range(N_PX):
                arrived(q, 0, q, 0)
                arrived(N_PX + q, 0, q, N_PY - 1)
            for q in range(N_PY):
                arrived(2 * N_PX + q, 0, 0, q)
                arrived(2 * N_PX + N_PY + q, 0, N_PX - 1, q)

        make_ring(s)
        for index in range(3):
            ag_copy(s, 1, index).start()
        for kind in range(2):
            for index in (1, 2):
                ag_copy(s, kind, index).wait_recv()
            for index in (5, 6):
                ag_copy(s, kind, index).start()
        for kind in range(2):
            ag_copy(s, kind, 0).wait_recv()
            for index in (3, 4):
                ag_copy(s, kind, index).start()
        for kind in range(2):
            for index in (3, 4):
                ag_copy(s, kind, index).wait_recv()
            for index in (7, 8):
                ag_copy(s, kind, index).start()
        for kind in range(2):
            for index in (5, 6, 7, 8):
                ag_copy(s, kind, index).wait_recv()

    def convolve(s):
        p = iota((CB, TILE), 1)
        a, b = p // RB, p % RB
        keep_a = (a >= 1, None, a < RA - 1)
        keep_b = (b >= 1, None, b < RB - 1)

        def face_conv(f, carry):
            y = dot(wst[s], held[s, f])
            total = None
            for dj in range(3):
                column = None
                for di in range(3):
                    tap = 3 * di + dj
                    term = y[CB * tap : CB * tap + CB, 0:TILE]
                    if di != 1:
                        term = pltpu.roll(term, (-(di - 1) * RB) % TILE, 1)
                        term = jnp.where(keep_a[di], term, 0.0)
                    column = term if column is None else column + term
                if dj != 1:
                    column = pltpu.roll(column, (-(dj - 1)) % TILE, 1)
                    column = jnp.where(keep_b[dj], column, 0.0)
                total = column if total is None else total + column
            pre[f] = total
            edge = jnp.concatenate(
                [y[CB * tap : CB * tap + CB, TILE:WIDE] for tap in range(9)], axis=1
            )
            high = edge.astype(BF16)
            ringy[f, 0:CB, :] = high
            ringy[f, CB : 2 * CB, :] = (edge - high.astype(F32)).astype(BF16)
            return carry

        lax.fori_loop(0, FACES, face_conv, 0)

        def add_ring(g, carry):
            first = pl.multiple_of(4 * g, 4)
            cells = ringy[pl.ds(first, 4)].reshape(8 * CB, 9 * RING)
            extra = dot(cells, sconv[...]).reshape(4, 2, CB, TILE)
            pre[pl.ds(first, 4)] += extra[:, 0] + extra[:, 1]
            return carry

        lax.fori_loop(0, FACES // 4, add_ring, 0)

    gather(0, feat_ref)
    convolve(0)

    def gate(f, carry):
        v = pre[f]
        sig = 1.0 / (1.0 + jnp.exp(-v))
        act_ref[f] = (v * sig).astype(BF16)
        gated[f] = (cot_ref[f].astype(F32) * sig * (1.0 + v * (1.0 - sig))).astype(BF16)
        return carry

    lax.fori_loop(0, FACES, gate, 0)
    gather(1, gated)
    convolve(1)

    def finish(f, carry):
        grad_ref[f] = pre[f].astype(BF16)
        return carry

    lax.fori_loop(0, FACES, finish, 0)

    for s in range(2):
        for kind in range(2):
            for index in range(9):
                ag_copy(s, kind, index).wait_send()
        for n, (dx, dy, kind, slot) in enumerate(HALO):

            @pl.when(inside(px + dx, py + dy))
            def _():
                halo_copy(s, n).wait_send()

        each_line_copy(s, lambda copy: copy.wait_send())


def local(features, cotangent, weight, edge_table, corner_table):
    def by_face(v):
        return jnp.transpose(v.reshape(CB, FACES, TILE), (1, 0, 2))

    vmem = pl.BlockSpec(memory_space=pltpu.VMEM)
    smem = pl.BlockSpec(memory_space=pltpu.SMEM)
    field = jax.ShapeDtypeStruct((FACES, CB, TILE), BF16)
    act, grad = pl.pallas_call(
        kernel,
        out_shape=(field, field),
        in_specs=[smem, smem, vmem, vmem, vmem],
        out_specs=(vmem, vmem),
        scratch_shapes=[
            pltpu.VMEM((2, FACES, 8 * CB, WIDE), BF16),
            pltpu.VMEM((2, 3, 3 * CB, 128), BF16),
            pltpu.VMEM((2, 8, 3 * CB, 128), BF16),
            pltpu.VMEM((2, 24, 3 * CB, 128), BF16),
            pltpu.VMEM((48, CB, 128), BF16),
            pltpu.VMEM((FACES, CB, RING), F32),
            pltpu.VMEM((FACES, CB, TILE), F32),
            pltpu.VMEM((FACES, 2 * CB, 9 * RING), BF16),
            pltpu.VMEM((FACES, CB, TILE), BF16),
            pltpu.VMEM((2, 9 * CB, 128), BF16),
            pltpu.VMEM((4, TILE, 384), BF16),
            pltpu.VMEM((1024, 512), BF16),
            pltpu.VMEM((512, 512), BF16),
            pltpu.VMEM((2, 1024, 512), BF16),
            pltpu.VMEM((9 * RING, TILE), BF16),
            pltpu.SemaphoreType.DMA((2, 2, 9)),
            pltpu.SemaphoreType.DMA((2, 2, 9)),
            pltpu.SemaphoreType.DMA((2, 8)),
            pltpu.SemaphoreType.DMA((2, 8)),
            pltpu.SemaphoreType.DMA((2, 4, N_PX * N_PY)),
            pltpu.SemaphoreType.DMA((2, 24)),
        ],
        compiler_params=pltpu.CompilerParams(
            collective_id=0, has_side_effects=True, vmem_limit_bytes=48 * 1024 * 1024
        ),
        name="conv_pair",
    )(
        edge_table.reshape(-1),
        corner_table.reshape(-1),
        by_face(features),
        by_face(cotangent),
        weight.reshape(9, 8 * CB, 8 * CB),
    )

    def by_channel(v):
        return jnp.transpose(v, (1, 0, 2)).reshape(CB, FACES, 1, 1, TILE)

    return by_channel(act), by_channel(grad)


def solution(mesh):
    field = P("ch", None, "py", "px", None)
    return jax.shard_map(
        local,
        mesh=mesh,
        in_specs=(field, field, P(), P(), P()),
        out_specs=(field, field),
        check_vma=False,
    )
```

```python
import functools

import jax
import jax.numpy as jnp
from jax import lax
from jax.experimental import pallas as pl
from jax.experimental.pallas import tpu as pltpu
from jax.sharding import PartitionSpec as P

MESH = pl.DeviceIdType.MESH
F32 = jnp.float32
BF16 = jnp.bfloat16
FACES, CB, RA, RB, TILE = 12, 16, 16, 32, 512
N_PX, N_PY, N_X, N_Z = 4, 8, 4, 2
SIDE = 128
RING = 128
WIDE = TILE + RING

TOP, BOTTOM, LEFT, RIGHT = 0, 34, 68, 84
HALO = (
    (0, 1, 1, 0),
    (0, -1, 0, 1),
    (1, 0, 2, 2),
    (-1, 0, 2, 3),
    (1, 1, 1, 4),
    (-1, 1, 1, 5),
    (1, -1, 0, 6),
    (-1, -1, 0, 7),
)
BORDER = tuple(
    (qx, qy)
    for qx in range(N_PX)
    for qy in range(N_PY)
    if qx in (0, N_PX - 1) or qy in (0, N_PY - 1)
)
SLOTS = 2 * N_PX + 2 * N_PY
PART = 3
PARTS = FACES // PART
Z, XU, XD, FU, FD, ZU, ZD, ZF = 0, 4, 5, 6, 7, 8, 12, 16


def iota(shape, dim):
    return lax.broadcasted_iota(jnp.int32, shape, dim)


def ones_where(mask):
    return jnp.where(mask, 1.0, 0.0).astype(BF16)


def dot(a, b):
    return jnp.dot(a, b, preferred_element_type=F32)


def fill_packers(px, py, sbd):
    p, n = iota((TILE, 128), 0), iota((TILE, 128), 1)
    i, j = n % 32, (n // 32 - px) & 3
    for kind in range(2):
        hit = p == (RA - 1) * RB * kind + i
        for k in range(4):
            sbd[k, :, 128 * kind : 128 * kind + 128] = ones_where(hit & (j == k))
    i, m = n % 16, (n // 16 - py) & 7
    hit = p == RB * i + jnp.where(m >= 4, RB - 1, 0)
    for k in range(4):
        sbd[k, :, 256:384] = ones_where(hit & ((m & 3) == k))


def fill_selectors(px, py, sring, sedge, scorner, sconv):
    row, m = iota((128, 128), 0), iota((128, 128), 1)
    i, j = row % 32, row // 32
    i16, item = row % 16, (row // 16 - py) & 7
    here, left, right = (j - px) & 3, (j - px + 1) & 3, (j - px - 1) & 3
    aims = (
        (here, TOP + 1 + i),
        (here, BOTTOM + 1 + i),
        (item & 3, jnp.where(item >= 4, LEFT + i16, -1)),
        (item & 3, jnp.where(item < 4, RIGHT + i16, -1)),
        (left, jnp.where(i == 31, TOP, -1)),
        (right, jnp.where(i == 0, TOP + 33, -1)),
        (left, jnp.where(i == 31, BOTTOM, -1)),
        (right, jnp.where(i == 0, BOTTOM + 33, -1)),
    )
    for slot, (k, aim) in enumerate(aims):
        for face in range(4):
            sring[128 * slot : 128 * slot + 128, 128 * face : 128 * face + 128] = ones_where(
                (k == face) & (m == aim)
            )
    none = jnp.full((128, 128), -1000, jnp.int32)
    for edge in range(4):
        if edge < 2:
            base = (TOP, BOTTOM)[edge]
            at = jnp.where((m >= base) & (m < base + 34), RB * px - 1 + m - base, none)
        else:
            base, shift = (LEFT, RIGHT)[edge - 2], 33 * (edge - 2)
            at = jnp.where((m >= base) & (m < base + 16), RA * py + m - base, none)
            at = jnp.where(m == TOP + shift, RA * py - 1, at)
            at = jnp.where(m == BOTTOM + shift, RA * py + RA, at)
        sedge[edge, :, 0:128] = ones_where(row == at)
        sedge[edge, :, 128:256] = ones_where(row == SIDE - 1 - at)
        cell = m == (TOP, TOP + 33, BOTTOM, BOTTOM + 33)[edge]
        scorner[edge, :, 0:128] = ones_where(cell & (row == 0))
        scorner[edge, :, 128:256] = ones_where(cell & (row == SIDE - 1))
    lane, p = iota((128, TILE), 0), iota((128, TILE), 1)
    for tap in range(9):
        pa, pb = p // RB + tap // 3, p % RB + tap % 3
        cell = jnp.where(
            pa == 0,
            TOP + pb,
            jnp.where(
                pa == RA + 1,
                BOTTOM + pb,
                jnp.where(pb == 0, LEFT + pa - 1, jnp.where(pb == RB + 1, RIGHT + pa - 1, -1)),
            ),
        )
        sconv[128 * tap : 128 * tap + 128, :] = ones_where(lane == cell)


def kernel(
    edge_ref,
    corner_ref,
    feat_ref,
    cot_hbm,
    w_hbm,
    act_ref,
    grad_ref,
    held,
    cot_ref,
    w_ref,
    bd,
    hal,
    lin,
    full,
    ring,
    pre,
    ringy,
    wst,
    sbd,
    sring,
    sedge,
    scorner,
    sconv,
    load_sem,
    ag_send,
    ag_recv,
    rg_send,
    rg_recv,
    halo_send,
    halo_recv,
    line_send,
    line_recv,
):
    px, py, ch = lax.axis_index("px"), lax.axis_index("py"), lax.axis_index("ch")
    z, x = ch // N_X, ch % N_X
    up_x = z * N_X + (x + 1) % N_X
    down_x = z * N_X + (x + N_X - 1) % N_X
    far = (1 - z) * N_X + x
    far_up = (1 - z) * N_X + (x + 1) % N_X
    far_down = (1 - z) * N_X + (x + N_X - 1) % N_X
    sides = (py == 0, py == N_PY - 1, px == 0, px == N_PX - 1)
    border = sides[0] | sides[1] | sides[2] | sides[3]
    at_corner = (sides[0] | sides[1]) & (sides[2] | sides[3])

    def rows(c):
        return pl.ds(pl.multiple_of(CB * c, CB), CB)

    loads = (
        pltpu.make_async_copy(feat_ref, held.at[0, :, rows(ch), pl.ds(0, TILE)], load_sem.at[0]),
        pltpu.make_async_copy(w_hbm, w_ref, load_sem.at[1]),
        pltpu.make_async_copy(cot_hbm, cot_ref, load_sem.at[2]),
    )
    for load in loads:
        load.start()

    barrier = pltpu.get_barrier_semaphore()

    def greet(t, carry):
        tx, ty = t // N_PY, t % N_PY

        @pl.when((tx != px) | (ty != py))
        def _():
            pl.semaphore_signal(barrier, inc=1, device_id={"px": tx, "py": ty}, device_id_type=MESH)

        return carry

    lax.fori_loop(0, N_PX * N_PY, greet, 0)
    for peer in (far, up_x, down_x):
        pl.semaphore_signal(barrier, inc=1, device_id={"ch": peer}, device_id_type=MESH)

    def pack(s):
        packed = None
        for k in range(4):
            part = jnp.concatenate(
                [held[s, 4 * q + k, rows(ch), 0:TILE] for q in range(3)], axis=0
            )
            term = dot(part, sbd[k])
            packed = term if packed is None else packed + term
        packed = packed.astype(BF16)
        for kind in range(3):
            bd[s, kind] = packed[:, 128 * kind : 128 * kind + 128]

    fill_packers(px, py, sbd)
    loads[0].wait()
    pack(0)
    fill_selectors(px, py, sring, sedge, scorner, sconv)
    loads[1].wait()
    pick_row = ones_where(iota((CB, 128), 1) == CB * ch + iota((CB, 128), 0))
    for tap in range(9):
        wst[0, CB * tap : CB * tap + CB, :] = w_ref[tap, rows(ch), :]
        wst[1, CB * tap : CB * tap + CB, :] = lax.dot_general(
            pick_row, w_ref[8 - tap], (((1,), (1,)), ((), ())), preferred_element_type=F32
        ).astype(BF16)
    for s in range(2):
        for dx, dy, kind, slot in HALO:
            sx, sy = px - dx, py - dy

            @pl.when((sx < 0) | (sx >= N_PX) | (sy < 0) | (sy >= N_PY))
            def _():
                hal[s, slot] = jnp.zeros((3 * CB, 128), BF16)

    loads[2].wait()
    pl.semaphore_wait(barrier, N_PX * N_PY - 1 + 3)

    def remote(ref, send, recv, device, dst=None):
        return pltpu.make_async_remote_copy(
            src_ref=ref,
            dst_ref=ref if dst is None else dst,
            send_sem=send,
            recv_sem=recv,
            device_id=device,
            device_id_type=MESH,
        )

    def ag_copy(s, index):
        if index < XU:
            block, target, first, count = ch, far, PART * index, PART
        elif index < ZU:
            block, target, first, count = (
                (ch, up_x, 0, FACES),
                (ch, down_x, 0, FACES),
                (down_x, up_x, 0, FACES // 2),
                (up_x, down_x, FACES // 2, FACES // 2),
            )[index - XU]
        elif index < ZF:
            part = (index - ZU) % 4
            block, target = far, up_x if index < ZD else down_x
            first, count = PART * part, PART
        else:
            part = index - ZF
            block, target = (far_down, up_x) if part < 2 else (far_up, down_x)
            first, count = PART * part, PART
        ref = held.at[s, pl.ds(first, count), rows(block), pl.ds(0, TILE)]
        return remote(ref, ag_send.at[s, index], ag_recv.at[s, index], {"ch": target})

    def rg_copy(s, index):
        block, target, first, count = (
            (ch, far, 0, 12),
            (ch, up_x, 0, 12),
            (ch, down_x, 0, 12),
            (far, up_x, 0, 12),
            (far, down_x, 0, 12),
            (down_x, up_x, 0, 6),
            (up_x, down_x, 6, 6),
            (far_down, up_x, 0, 6),
            (far_up, down_x, 6, 6),
        )[index]
        ref = held.at[s, pl.ds(first, count), rows(block), pl.ds(TILE, RING)]
        return remote(ref, rg_send.at[s, index], rg_recv.at[s, index], {"ch": target})

    def halo_copy(s, n):
        dx, dy, kind, slot = HALO[n]
        return remote(
            bd.at[s, kind],
            halo_send.at[s, slot],
            halo_recv.at[s, slot],
            {"px": px + dx, "py": py + dy},
            hal.at[s, slot],
        )

    def inside(qx, qy):
        return (qx >= 0) & (qx < N_PX) & (qy >= 0) & (qy < N_PY)

    my_slots = (px, N_PX + px, 2 * N_PX + py, 2 * N_PX + N_PY + py)

    def many_lines(s, count, send, recv):
        ref = lin.at[s, pl.ds(0, count)]
        return remote(ref, send, recv, {"px": px, "py": py})

    def send_lines(s):
        for side in range(4):

            @pl.when(sides[side])
            def _():
                for tx, ty in BORDER:

                    @pl.when((px != tx) | (py != ty))
                    def _():
                        remote(
                            bd.at[s, min(side, 2)],
                            line_send.at[s, side],
                            line_recv.at[s],
                            {"px": tx, "py": ty},
                            lin.at[s, my_slots[side]],
                        ).start()

                lin[s, my_slots[side]] = bd[s, min(side, 2)]

    def take_lines(s):
        @pl.when(at_corner)
        def _():
            many_lines(s, SLOTS - 2, line_send.at[s, 0], line_recv.at[s]).wait_recv()

        @pl.when(border & jnp.logical_not(at_corner))
        def _():
            many_lines(s, SLOTS - 1, line_send.at[s, 0], line_recv.at[s]).wait_recv()

    def make_ring(s):
        cells = jnp.concatenate([hal[s, slot] for slot in range(8)], axis=1)
        inner = dot(cells, sring[...])
        for q in range(3):
            for k in range(4):
                ring[4 * q + k] = inner[CB * q : CB * q + CB, 128 * k : 128 * k + 128]

        @pl.when(border)
        def _():
            lane = iota((3 * CB, 128), 1)
            for side in range(4):
                first, count, width, item = (
                    (0, N_PX, 32, 0),
                    (N_PX, N_PX, 32, 0),
                    (2 * N_PX, N_PY, 16, 0),
                    (2 * N_PX + N_PY, N_PY, 16, 4),
                )[side]
                parts = [lin[s, first + q].astype(F32) for q in range(count)]
                for k in range(4):
                    line = parts[0]
                    for q in range(1, count):
                        line = jnp.where(
                            lane // width == (item + k + q) % count, parts[q], line
                        )
                    turn = (-width * (item + k)) % 128
                    if turn:
                        line = pltpu.roll(line, turn, 1)
                    line = line.astype(BF16)
                    for q in range(3):
                        full[12 * side + 4 * q + k] = line[CB * q : CB * q + CB, :]
            for edge in range(4):

                @pl.when(sides[edge])
                def _():
                    found = jnp.concatenate(
                        [full[12 * edge_ref[1, edge, f] + edge_ref[0, edge, f]] for f in range(FACES)],
                        axis=0,
                    )
                    both = dot(found, sedge[edge])
                    for f in range(FACES):
                        mine = both[CB * f : CB * f + CB]
                        ring[f] += jnp.where(
                            edge_ref[2, edge, f] == 1, mine[:, 128:256], mine[:, 0:128]
                        )

            for corner in range(4):

                @pl.when(sides[corner // 2] & sides[2 + corner % 2])
                def _():
                    found = jnp.concatenate(
                        [
                            full[12 * (corner_ref[corner, 1, f] // 2) + corner_ref[corner, 0, f]]
                            for f in range(FACES)
                        ],
                        axis=0,
                    )
                    both = dot(found, scorner[corner])
                    for f in range(FACES):
                        mine = both[CB * f : CB * f + CB]
                        ring[f] += jnp.where(
                            corner_ref[corner, 1, f] % 2 == 1, mine[:, 128:256], mine[:, 0:128]
                        )

        held[s, :, rows(ch), TILE:WIDE] = ring[...].astype(BF16)

    p = iota((CB, TILE), 1)
    a, b = p // RB, p % RB
    keep_a = (a >= 1, None, a < RA - 1)
    keep_b = (b >= 1, None, b < RB - 1)

    def inner_conv(s, part):
        for f in range(PART * part, PART * part + PART):
            y = dot(wst[s], held[s, f, :, 0:TILE])
            total = None
            for dj in range(3):
                column = None
                for di in range(3):
                    tap = 3 * di + dj
                    term = y[CB * tap : CB * tap + CB]
                    if di != 1:
                        term = pltpu.roll(term, (-(di - 1) * RB) % TILE, 1)
                        term = jnp.where(keep_a[di], term, 0.0)
                    column = term if column is None else column + term
                if dj != 1:
                    column = pltpu.roll(column, (-(dj - 1)) % TILE, 1)
                    column = jnp.where(keep_b[dj], column, 0.0)
                total = column if total is None else total + column
            pre[f] = total

    def ring_conv(s):
        for f in range(FACES):
            y = dot(wst[s], held[s, f, :, TILE:WIDE])
            edge = jnp.concatenate([y[CB * tap : CB * tap + CB] for tap in range(9)], axis=1)
            high = edge.astype(BF16)
            ringy[f, 0:CB, :] = high
            ringy[f, CB : 2 * CB, :] = (edge - high.astype(F32)).astype(BF16)

        def add_ring(g, carry):
            first = pl.multiple_of(4 * g, 4)
            cells = ringy[pl.ds(first, 4)].reshape(8 * CB, 9 * RING)
            extra = dot(cells, sconv[...]).reshape(4, 2, CB, TILE)
            v = pre[pl.ds(first, 4)] + extra[:, 0] + extra[:, 1]
            if s == 0:
                sig = 1.0 / (1.0 + jnp.exp(-v))
                act_ref[pl.ds(first, 4)] = (v * sig).astype(BF16)
                slope = cot_ref[pl.ds(first, 4)].astype(F32) * sig * (1.0 + v * (1.0 - sig))
                held[1, pl.ds(first, 4), rows(ch), 0:TILE] = slope.astype(BF16)
            else:
                grad_ref[pl.ds(first, 4)] = v.astype(BF16)
            return carry

        lax.fori_loop(0, FACES // 4, add_ring, 0)

    for s in range(2):
        if s == 1:
            pack(1)
        for n, (dx, dy, kind, slot) in enumerate(HALO):

            @pl.when(inside(px + dx, py + dy))
            def _():
                halo_copy(s, n).start()

        send_lines(s)
        for index in (Z, XU, XD, Z + 1, Z + 2, Z + 3):
            ag_copy(s, index).start()

        def came(*indices):
            for index in indices:
                ag_copy(s, index).wait_recv()

        def go(*indices):
            for index in indices:
                ag_copy(s, index).start()

        def ring_came(*indices):
            for index in indices:
                rg_copy(s, index).wait_recv()

        def ring_go(*indices):
            for index in indices:
                rg_copy(s, index).start()

        came(XU, XD)
        go(FU, FD)
        came(Z)
        go(ZU, ZD)
        came(Z + 1)
        go(ZU + 1, ZD + 1)
        for n, (dx, dy, kind, slot) in enumerate(HALO):

            @pl.when(inside(px - dx, py - dy))
            def _():
                halo_copy(s, n).wait_recv()

        take_lines(s)
        make_ring(s)
        ring_go(0, 1, 2)
        came(Z + 2)
        go(ZU + 2, ZD + 2)
        came(Z + 3)
        go(ZU + 3, ZD + 3)
        came(ZU)
        go(ZF)
        came(ZU + 1)
        go(ZF + 1)
        ring_came(1, 2)
        ring_go(5, 6)
        ring_came(0)
        ring_go(3, 4)
        came(ZD + 2)
        go(ZF + 2)
        came(ZD + 3)
        go(ZF + 3)
        came(FU, FD, ZD, ZF)
        inner_conv(s, 0)
        ring_came(3, 4)
        ring_go(7, 8)
        came(ZD + 1, ZF + 1)
        inner_conv(s, 1)
        came(ZU + 2, ZF + 2)
        inner_conv(s, 2)
        came(ZU + 3, ZF + 3)
        inner_conv(s, 3)
        ring_came(5, 6, 7, 8)
        ring_conv(s)

    for s in range(2):
        for index in range(ZF + 4):
            ag_copy(s, index).wait_send()
        for index in range(9):
            rg_copy(s, index).wait_send()
        for n, (dx, dy, kind, slot) in enumerate(HALO):

            @pl.when(inside(px + dx, py + dy))
            def _():
                halo_copy(s, n).wait_send()

        for side in range(4):

            @pl.when(sides[side])
            def _():
                many_lines(s, len(BORDER) - 1, line_send.at[s, side], line_recv.at[s]).wait_send()


def local(features, cotangent, weight, edge_table, corner_table):
    def by_face(v):
        return jnp.transpose(v.reshape(CB, FACES, TILE), (1, 0, 2))

    vmem = pl.BlockSpec(memory_space=pltpu.VMEM)
    smem = pl.BlockSpec(memory_space=pltpu.SMEM)
    hbm = pl.BlockSpec(memory_space=pl.ANY)
    field = jax.ShapeDtypeStruct((FACES, CB, TILE), BF16)
    act, grad = pl.pallas_call(
        kernel,
        out_shape=(field, field),
        in_specs=[smem, smem, hbm, hbm, hbm],
        out_specs=(vmem, vmem),
        scratch_shapes=[
            pltpu.VMEM((2, FACES, 8 * CB, WIDE), BF16),
            pltpu.VMEM((FACES, CB, TILE), BF16),
            pltpu.VMEM((9, 8 * CB, 8 * CB), BF16),
            pltpu.VMEM((2, 3, 3 * CB, 128), BF16),
            pltpu.VMEM((2, 8, 3 * CB, 128), BF16),
            pltpu.VMEM((2, SLOTS, 3 * CB, 128), BF16),
            pltpu.VMEM((48, CB, 128), BF16),
            pltpu.VMEM((FACES, CB, RING), F32),
            pltpu.VMEM((FACES, CB, TILE), F32),
            pltpu.VMEM((FACES, 2 * CB, 9 * RING), BF16),
            pltpu.VMEM((2, 9 * CB, 128), BF16),
            pltpu.VMEM((4, TILE, 384), BF16),
            pltpu.VMEM((1024, 512), BF16),
            pltpu.VMEM((4, 128, 256), BF16),
            pltpu.VMEM((4, 128, 256), BF16),
            pltpu.VMEM((9 * RING, TILE), BF16),
            pltpu.SemaphoreType.DMA((3,)),
            pltpu.SemaphoreType.DMA((2, ZF + 4)),
            pltpu.SemaphoreType.DMA((2, ZF + 4)),
            pltpu.SemaphoreType.DMA((2, 9)),
            pltpu.SemaphoreType.DMA((2, 9)),
            pltpu.SemaphoreType.DMA((2, 8)),
            pltpu.SemaphoreType.DMA((2, 8)),
            pltpu.SemaphoreType.DMA((2, 4)),
            pltpu.SemaphoreType.DMA((2,)),
        ],
        compiler_params=pltpu.CompilerParams(
            collective_id=0, has_side_effects=True, vmem_limit_bytes=56 * 1024 * 1024
        ),
        name="conv_pair",
    )(
        jnp.transpose(edge_table, (2, 1, 0)),
        jnp.transpose(corner_table, (1, 2, 0)),
        by_face(features),
        by_face(cotangent),
        weight.reshape(9, 8 * CB, 8 * CB),
    )

    def by_channel(v):
        return jnp.transpose(v, (1, 0, 2)).reshape(CB, FACES, 1, 1, TILE)

    return by_channel(act), by_channel(grad)


def solution(mesh):
    field = P("ch", None, "py", "px", None)
    return jax.shard_map(
        local,
        mesh=mesh,
        in_specs=(field, field, P(), P(), P()),
        out_specs=(field, field),
        check_vma=False,
    )
```

```python
import functools

import jax
import jax.numpy as jnp
from jax import lax
from jax.experimental import pallas as pl
from jax.experimental.pallas import tpu as pltpu
from jax.sharding import PartitionSpec as P

MESH = pl.DeviceIdType.MESH
F32 = jnp.float32
BF16 = jnp.bfloat16
FACES, CB, RA, RB, TILE = 12, 16, 16, 32, 512
N_PX, N_PY, N_X, N_Z = 4, 8, 4, 2
SIDE = 128
RING = 128
WIDE = TILE + RING

TOP, BOTTOM, LEFT, RIGHT = 0, 34, 68, 84
HALO = (
    (0, 1, 1, 0),
    (0, -1, 0, 1),
    (1, 0, 2, 2),
    (-1, 0, 2, 3),
    (1, 1, 1, 4),
    (-1, 1, 1, 5),
    (1, -1, 0, 6),
    (-1, -1, 0, 7),
)
BORDER = tuple(
    (qx, qy)
    for qx in range(N_PX)
    for qy in range(N_PY)
    if qx in (0, N_PX - 1) or qy in (0, N_PY - 1)
)
SLOTS = 2 * N_PX + 2 * N_PY
PARTS = ((0, 3), (3, 3), (6, 3), (9, 3))
Z, XU, XD, FU, FD, ZU, ZD, ZF = 0, 4, 5, 6, 7, 8, 12, 16


def iota(shape, dim):
    return lax.broadcasted_iota(jnp.int32, shape, dim)


def ones_where(mask):
    return jnp.where(mask, 1.0, 0.0).astype(BF16)


def dot(a, b):
    return jnp.dot(a, b, preferred_element_type=F32)


def fill_packers(px, py, sbd):
    p, n = iota((TILE, 128), 0), iota((TILE, 128), 1)
    i, j = n % 32, (n // 32 - px) & 3
    for kind in range(2):
        hit = p == (RA - 1) * RB * kind + i
        for k in range(4):
            sbd[k, :, 128 * kind : 128 * kind + 128] = ones_where(hit & (j == k))
    i, m = n % 16, (n // 16 - py) & 7
    hit = p == RB * i + jnp.where(m >= 4, RB - 1, 0)
    for k in range(4):
        sbd[k, :, 256:384] = ones_where(hit & ((m & 3) == k))


def fill_selectors(px, py, sring, sedge, scorner, sconv):
    row, m = iota((128, 128), 0), iota((128, 128), 1)
    i, j = row % 32, row // 32
    i16, item = row % 16, (row // 16 - py) & 7
    here, left, right = (j - px) & 3, (j - px + 1) & 3, (j - px - 1) & 3
    aims = (
        (here, TOP + 1 + i),
        (here, BOTTOM + 1 + i),
        (item & 3, jnp.where(item >= 4, LEFT + i16, -1)),
        (item & 3, jnp.where(item < 4, RIGHT + i16, -1)),
        (left, jnp.where(i == 31, TOP, -1)),
        (right, jnp.where(i == 0, TOP + 33, -1)),
        (left, jnp.where(i == 31, BOTTOM, -1)),
        (right, jnp.where(i == 0, BOTTOM + 33, -1)),
    )
    for slot, (k, aim) in enumerate(aims):
        for face in range(4):
            sring[128 * slot : 128 * slot + 128, 128 * face : 128 * face + 128] = ones_where(
                (k == face) & (m == aim)
            )
    none = jnp.full((128, 128), -1000, jnp.int32)
    for edge in range(4):
        if edge < 2:
            base = (TOP, BOTTOM)[edge]
            at = jnp.where((m >= base) & (m < base + 34), RB * px - 1 + m - base, none)
        else:
            base, shift = (LEFT, RIGHT)[edge - 2], 33 * (edge - 2)
            at = jnp.where((m >= base) & (m < base + 16), RA * py + m - base, none)
            at = jnp.where(m == TOP + shift, RA * py - 1, at)
            at = jnp.where(m == BOTTOM + shift, RA * py + RA, at)
        sedge[edge, :, 0:128] = ones_where(row == at)
        sedge[edge, :, 128:256] = ones_where(row == SIDE - 1 - at)
        cell = m == (TOP, TOP + 33, BOTTOM, BOTTOM + 33)[edge]
        scorner[edge, :, 0:128] = ones_where(cell & (row == 0))
        scorner[edge, :, 128:256] = ones_where(cell & (row == SIDE - 1))
    lane, p = iota((128, TILE), 0), iota((128, TILE), 1)
    for tap in range(9):
        pa, pb = p // RB + tap // 3, p % RB + tap % 3
        cell = jnp.where(
            pa == 0,
            TOP + pb,
            jnp.where(
                pa == RA + 1,
                BOTTOM + pb,
                jnp.where(pb == 0, LEFT + pa - 1, jnp.where(pb == RB + 1, RIGHT + pa - 1, -1)),
            ),
        )
        sconv[128 * tap : 128 * tap + 128, :] = ones_where(lane == cell)


def kernel(
    edge_ref,
    corner_ref,
    feat_ref,
    cot_hbm,
    w_hbm,
    act_hbm,
    grad_hbm,
    held,
    act_ref,
    grad_ref,
    cot_ref,
    w_ref,
    bd,
    hal,
    lin,
    full,
    ring,
    pre,
    ringy,
    wst,
    sbd,
    sring,
    sedge,
    scorner,
    sconv,
    load_sem,
    ag_send,
    ag_recv,
    rg_send,
    rg_recv,
    halo_send,
    halo_recv,
    line_send,
    line_recv,
):
    px, py, ch = lax.axis_index("px"), lax.axis_index("py"), lax.axis_index("ch")
    z, x = ch // N_X, ch % N_X
    up_x = z * N_X + (x + 1) % N_X
    down_x = z * N_X + (x + N_X - 1) % N_X
    far = (1 - z) * N_X + x
    opp_x = z * N_X + (x + 2) % N_X
    far_up = (1 - z) * N_X + (x + 1) % N_X
    far_down = (1 - z) * N_X + (x + N_X - 1) % N_X
    sides = (py == 0, py == N_PY - 1, px == 0, px == N_PX - 1)
    border = sides[0] | sides[1] | sides[2] | sides[3]
    at_corner = (sides[0] | sides[1]) & (sides[2] | sides[3])

    def rows(c):
        return pl.ds(pl.multiple_of(CB * c, CB), CB)

    loads = (
        pltpu.make_async_copy(feat_ref, held.at[0, :, rows(ch), pl.ds(0, TILE)], load_sem.at[0]),
        pltpu.make_async_copy(w_hbm, w_ref, load_sem.at[1]),
        pltpu.make_async_copy(cot_hbm, cot_ref, load_sem.at[2]),
    )
    for load in loads:
        load.start()
    keep_act = pltpu.make_async_copy(act_ref, act_hbm, load_sem.at[3])

    def keep_grad(g):
        part = pl.ds(pl.multiple_of(4 * g, 4), 4)
        return pltpu.make_async_copy(grad_ref.at[part], grad_hbm.at[part], load_sem.at[4 + g])

    barrier = pltpu.get_barrier_semaphore()

    def greet(t, carry):
        tx, ty = t // N_PY, t % N_PY

        @pl.when((tx != px) | (ty != py))
        def _():
            pl.semaphore_signal(barrier, inc=1, device_id={"px": tx, "py": ty}, device_id_type=MESH)

        return carry

    lax.fori_loop(0, N_PX * N_PY, greet, 0)
    for peer in (far, up_x, down_x, opp_x):
        pl.semaphore_signal(barrier, inc=1, device_id={"ch": peer}, device_id_type=MESH)

    def pack(s):
        packed = None
        for k in range(4):
            part = jnp.concatenate(
                [held[s, 4 * q + k, rows(ch), 0:TILE] for q in range(3)], axis=0
            )
            term = dot(part, sbd[k])
            packed = term if packed is None else packed + term
        packed = packed.astype(BF16)
        for kind in range(3):
            bd[s, kind] = packed[:, 128 * kind : 128 * kind + 128]

    fill_packers(px, py, sbd)
    loads[0].wait()
    pack(0)
    fill_selectors(px, py, sring, sedge, scorner, sconv)
    loads[1].wait()
    pick_row = ones_where(iota((CB, 128), 1) == CB * ch + iota((CB, 128), 0))
    for tap in range(9):
        wst[0, CB * tap : CB * tap + CB, :] = w_ref[tap, rows(ch), :]
        wst[1, CB * tap : CB * tap + CB, :] = lax.dot_general(
            pick_row, w_ref[8 - tap], (((1,), (1,)), ((), ())), preferred_element_type=F32
        ).astype(BF16)
    for s in range(2):
        for dx, dy, kind, slot in HALO:
            sx, sy = px - dx, py - dy

            @pl.when((sx < 0) | (sx >= N_PX) | (sy < 0) | (sy >= N_PY))
            def _():
                hal[s, slot] = jnp.zeros((3 * CB, 128), BF16)

    loads[2].wait()
    pl.semaphore_wait(barrier, N_PX * N_PY - 1 + 4)

    def remote(ref, send, recv, device, dst=None):
        return pltpu.make_async_remote_copy(
            src_ref=ref,
            dst_ref=ref if dst is None else dst,
            send_sem=send,
            recv_sem=recv,
            device_id=device,
            device_id_type=MESH,
        )

    def ag_copy(s, index):
        if index < XU:
            block, target, (first, count) = ch, far, PARTS[index]
        elif index < ZU:
            block, target, first, count = (
                (ch, up_x, 0, FACES),
                (ch, down_x, 0, FACES),
                (down_x, up_x, 0, FACES // 2),
                (up_x, down_x, FACES // 2, FACES // 2),
            )[index - XU]
        elif index < ZF:
            part = (index - ZU) % 4
            block, target, (first, count) = far, up_x if index < ZD else down_x, PARTS[part]
        else:
            part = index - ZF
            block, target = ((far_down, up_x), (far_up, down_x), (far, opp_x), (far, opp_x))[part]
            first, count = PARTS[part]
        ref = held.at[s, pl.ds(first, count), rows(block), pl.ds(0, TILE)]
        return remote(ref, ag_send.at[s, index], ag_recv.at[s, index], {"ch": target})

    def rg_copy(s, index):
        block, target, first, count = (
            (ch, far, 0, 12),
            (ch, up_x, 0, 12),
            (ch, down_x, 0, 12),
            (far, up_x, 0, 12),
            (far, down_x, 0, 12),
            (ch, opp_x, 0, 12),
            (far, opp_x, 0, 12),
        )[index]
        ref = held.at[s, pl.ds(first, count), rows(block), pl.ds(TILE, RING)]
        return remote(ref, rg_send.at[s, index], rg_recv.at[s, index], {"ch": target})

    def halo_copy(s, n):
        dx, dy, kind, slot = HALO[n]
        return remote(
            bd.at[s, kind],
            halo_send.at[s, slot],
            halo_recv.at[s, slot],
            {"px": px + dx, "py": py + dy},
            hal.at[s, slot],
        )

    def inside(qx, qy):
        return (qx >= 0) & (qx < N_PX) & (qy >= 0) & (qy < N_PY)

    my_slots = (px, N_PX + px, 2 * N_PX + py, 2 * N_PX + N_PY + py)

    def many_lines(s, count, send, recv):
        ref = lin.at[s, pl.ds(0, count)]
        return remote(ref, send, recv, {"px": px, "py": py})

    def send_lines(s):
        for side in range(4):

            @pl.when(sides[side])
            def _():
                for tx, ty in BORDER:

                    @pl.when((px != tx) | (py != ty))
                    def _():
                        remote(
                            bd.at[s, min(side, 2)],
                            line_send.at[s, side],
                            line_recv.at[s],
                            {"px": tx, "py": ty},
                            lin.at[s, my_slots[side]],
                        ).start()

                lin[s, my_slots[side]] = bd[s, min(side, 2)]

    def take_lines(s):
        @pl.when(at_corner)
        def _():
            many_lines(s, SLOTS - 2, line_send.at[s, 0], line_recv.at[s]).wait_recv()

        @pl.when(border & jnp.logical_not(at_corner))
        def _():
            many_lines(s, SLOTS - 1, line_send.at[s, 0], line_recv.at[s]).wait_recv()

    def make_ring(s):
        cells = jnp.concatenate([hal[s, slot] for slot in range(8)], axis=1)
        inner = dot(cells, sring[...])
        for q in range(3):
            for k in range(4):
                ring[4 * q + k] = inner[CB * q : CB * q + CB, 128 * k : 128 * k + 128]

        @pl.when(border)
        def _():
            lane = iota((3 * CB, 128), 1)
            for side in range(4):
                first, count, width, item = (
                    (0, N_PX, 32, 0),
                    (N_PX, N_PX, 32, 0),
                    (2 * N_PX, N_PY, 16, 0),
                    (2 * N_PX + N_PY, N_PY, 16, 4),
                )[side]
                parts = [lin[s, first + q].astype(F32) for q in range(count)]
                for k in range(4):
                    line = parts[0]
                    for q in range(1, count):
                        line = jnp.where(
                            lane // width == (item + k + q) % count, parts[q], line
                        )
                    turn = (-width * (item + k)) % 128
                    if turn:
                        line = pltpu.roll(line, turn, 1)
                    line = line.astype(BF16)
                    for q in range(3):
                        full[12 * side + 4 * q + k] = line[CB * q : CB * q + CB, :]
            for edge in range(4):

                @pl.when(sides[edge])
                def _():
                    found = jnp.concatenate(
                        [full[12 * edge_ref[1, edge, f] + edge_ref[0, edge, f]] for f in range(FACES)],
                        axis=0,
                    )
                    both = dot(found, sedge[edge])
                    for f in range(FACES):
                        mine = both[CB * f : CB * f + CB]
                        ring[f] += jnp.where(
                            edge_ref[2, edge, f] == 1, mine[:, 128:256], mine[:, 0:128]
                        )

            for corner in range(4):

                @pl.when(sides[corner // 2] & sides[2 + corner % 2])
                def _():
                    found = jnp.concatenate(
                        [
                            full[12 * (corner_ref[corner, 1, f] // 2) + corner_ref[corner, 0, f]]
                            for f in range(FACES)
                        ],
                        axis=0,
                    )
                    both = dot(found, scorner[corner])
                    for f in range(FACES):
                        mine = both[CB * f : CB * f + CB]
                        ring[f] += jnp.where(
                            corner_ref[corner, 1, f] % 2 == 1, mine[:, 128:256], mine[:, 0:128]
                        )

        held[s, :, rows(ch), TILE:WIDE] = ring[...].astype(BF16)

    p = iota((CB, TILE), 1)
    a, b = p // RB, p % RB
    keep_a = (a >= 1, None, a < RA - 1)
    keep_b = (b >= 1, None, b < RB - 1)

    def inner_conv(s, part):
        for f in range(PARTS[part][0], sum(PARTS[part])):
            y = dot(wst[s], held[s, f, :, 0:TILE])
            total = None
            for dj in range(3):
                column = None
                for di in range(3):
                    tap = 3 * di + dj
                    term = y[CB * tap : CB * tap + CB]
                    if di != 1:
                        term = pltpu.roll(term, (-(di - 1) * RB) % TILE, 1)
                        term = jnp.where(keep_a[di], term, 0.0)
                    column = term if column is None else column + term
                if dj != 1:
                    column = pltpu.roll(column, (-(dj - 1)) % TILE, 1)
                    column = jnp.where(keep_b[dj], column, 0.0)
                total = column if total is None else total + column
            pre[f] = total

    def ring_conv(s):
        for f in range(FACES):
            y = dot(wst[s], held[s, f, :, TILE:WIDE])
            edge = jnp.concatenate([y[CB * tap : CB * tap + CB] for tap in range(9)], axis=1)
            high = edge.astype(BF16)
            ringy[f, 0:CB, :] = high
            ringy[f, CB : 2 * CB, :] = (edge - high.astype(F32)).astype(BF16)

        def add_ring(g, carry):
            first = pl.multiple_of(4 * g, 4)
            cells = ringy[pl.ds(first, 4)].reshape(8 * CB, 9 * RING)
            extra = dot(cells, sconv[...]).reshape(4, 2, CB, TILE)
            v = pre[pl.ds(first, 4)] + extra[:, 0] + extra[:, 1]
            if s == 0:
                sig = 1.0 / (1.0 + jnp.exp(-v))
                act_ref[pl.ds(first, 4)] = (v * sig).astype(BF16)
                slope = cot_ref[pl.ds(first, 4)].astype(F32) * sig * (1.0 + v * (1.0 - sig))
                held[1, pl.ds(first, 4), rows(ch), 0:TILE] = slope.astype(BF16)
            else:
                grad_ref[pl.ds(first, 4)] = v.astype(BF16)
                keep_grad(g).start()
            return carry

        lax.fori_loop(0, FACES // 4, add_ring, 0)
        if s == 0:
            keep_act.start()

    for s in range(2):
        if s == 1:
            pack(1)
        for n, (dx, dy, kind, slot) in enumerate(HALO):

            @pl.when(inside(px + dx, py + dy))
            def _():
                halo_copy(s, n).start()

        send_lines(s)
        for index in (Z, XU, XD):
            ag_copy(s, index).start()

        def sent(*indices):
            for index in indices:
                ag_copy(s, index).wait_send()

        def came(*indices):
            for index in indices:
                ag_copy(s, index).wait_recv()

        def go(*indices):
            for index in indices:
                ag_copy(s, index).start()

        def ring_came(*indices):
            for index in indices:
                rg_copy(s, index).wait_recv()

        def ring_go(*indices):
            for index in indices:
                rg_copy(s, index).start()

        sent(Z)
        go(Z + 1)
        sent(Z + 1)
        go(Z + 2)
        came(XU, XD)
        go(FU, FD)
        came(Z)
        go(ZU, ZD)
        sent(Z + 2)
        go(Z + 3)
        came(Z + 1)
        go(ZU + 1, ZD + 1)
        for n, (dx, dy, kind, slot) in enumerate(HALO):

            @pl.when(inside(px - dx, py - dy))
            def _():
                halo_copy(s, n).wait_recv()

        take_lines(s)
        make_ring(s)
        ring_go(0, 1, 2, 5)
        came(Z + 2)
        go(ZU + 2, ZD + 2, ZF + 2)
        came(ZU)
        go(ZF)
        came(ZD + 1)
        go(ZF + 1)
        came(Z + 3)
        go(ZU + 3, ZD + 3, ZF + 3)
        ring_came(0)
        ring_go(3, 4, 6)
        came(FU, FD, ZD, ZF)
        inner_conv(s, 0)
        came(ZU + 1, ZF + 1)
        inner_conv(s, 1)
        came(ZU + 2, ZD + 2, ZF + 2)
        inner_conv(s, 2)
        came(ZU + 3, ZD + 3, ZF + 3)
        inner_conv(s, 3)
        ring_came(1, 2, 3, 4, 5, 6)
        ring_conv(s)

    for s in range(2):
        for index in range(Z + 3, ZF + 4):
            ag_copy(s, index).wait_send()
        for index in range(7):
            rg_copy(s, index).wait_send()
        for n, (dx, dy, kind, slot) in enumerate(HALO):

            @pl.when(inside(px + dx, py + dy))
            def _():
                halo_copy(s, n).wait_send()

        for side in range(4):

            @pl.when(sides[side])
            def _():
                many_lines(s, len(BORDER) - 1, line_send.at[s, side], line_recv.at[s]).wait_send()

    keep_act.wait()
    for g in range(FACES // 4):
        keep_grad(g).wait()


def local(features, cotangent, weight, edge_table, corner_table):
    def by_face(v):
        return jnp.transpose(v.reshape(CB, FACES, TILE), (1, 0, 2))

    smem = pl.BlockSpec(memory_space=pltpu.SMEM)
    hbm = pl.BlockSpec(memory_space=pl.ANY)
    field = jax.ShapeDtypeStruct((FACES, CB, TILE), BF16)
    act, grad = pl.pallas_call(
        kernel,
        out_shape=(field, field),
        in_specs=[smem, smem, hbm, hbm, hbm],
        out_specs=(hbm, hbm),
        scratch_shapes=[
            pltpu.VMEM((2, FACES, 8 * CB, WIDE), BF16),
            pltpu.VMEM((FACES, CB, TILE), BF16),
            pltpu.VMEM((FACES, CB, TILE), BF16),
            pltpu.VMEM((FACES, CB, TILE), BF16),
            pltpu.VMEM((9, 8 * CB, 8 * CB), BF16),
            pltpu.VMEM((2, 3, 3 * CB, 128), BF16),
            pltpu.VMEM((2, 8, 3 * CB, 128), BF16),
            pltpu.VMEM((2, SLOTS, 3 * CB, 128), BF16),
            pltpu.VMEM((48, CB, 128), BF16),
            pltpu.VMEM((FACES, CB, RING), F32),
            pltpu.VMEM((FACES, CB, TILE), F32),
            pltpu.VMEM((FACES, 2 * CB, 9 * RING), BF16),
            pltpu.VMEM((2, 9 * CB, 128), BF16),
            pltpu.VMEM((4, TILE, 384), BF16),
            pltpu.VMEM((1024, 512), BF16),
            pltpu.VMEM((4, 128, 256), BF16),
            pltpu.VMEM((4, 128, 256), BF16),
            pltpu.VMEM((9 * RING, TILE), BF16),
            pltpu.SemaphoreType.DMA((7,)),
            pltpu.SemaphoreType.DMA((2, ZF + 4)),
            pltpu.SemaphoreType.DMA((2, ZF + 4)),
            pltpu.SemaphoreType.DMA((2, 9)),
            pltpu.SemaphoreType.DMA((2, 9)),
            pltpu.SemaphoreType.DMA((2, 8)),
            pltpu.SemaphoreType.DMA((2, 8)),
            pltpu.SemaphoreType.DMA((2, 4)),
            pltpu.SemaphoreType.DMA((2,)),
        ],
        compiler_params=pltpu.CompilerParams(
            collective_id=0, has_side_effects=True, vmem_limit_bytes=56 * 1024 * 1024
        ),
        name="conv_pair",
    )(
        jnp.transpose(edge_table, (2, 1, 0)),
        jnp.transpose(corner_table, (1, 2, 0)),
        by_face(features),
        by_face(cotangent),
        weight.reshape(9, 8 * CB, 8 * CB),
    )

    def by_channel(v):
        return jnp.transpose(v, (1, 0, 2)).reshape(CB, FACES, 1, 1, TILE)

    return by_channel(act), by_channel(grad)


def solution(mesh):
    field = P("ch", None, "py", "px", None)
    return jax.shard_map(
        local,
        mesh=mesh,
        in_specs=(field, field, P(), P(), P()),
        out_specs=(field, field),
        check_vma=False,
    )
```

```python
import functools

import jax
import jax.numpy as jnp
from jax import lax
from jax.experimental import pallas as pl
from jax.experimental.pallas import tpu as pltpu
from jax.sharding import PartitionSpec as P

MESH = pl.DeviceIdType.MESH
F32 = jnp.float32
BF16 = jnp.bfloat16
FACES, CB, RA, RB, TILE = 12, 16, 16, 32, 512
N_PX, N_PY, N_X, N_Z = 4, 8, 4, 2
SIDE = 128
RING = 128
WIDE = TILE + RING

TOP, BOTTOM, LEFT, RIGHT = 0, 34, 68, 84
HALO = (
    (0, 1, 1, 0),
    (0, -1, 0, 1),
    (1, 0, 2, 2),
    (-1, 0, 2, 3),
    (1, 1, 1, 4),
    (-1, 1, 1, 5),
    (1, -1, 0, 6),
    (-1, -1, 0, 7),
)
LONE = ((1, 0), (2, 0), (1, N_PY - 1), (2, N_PY - 1))
FANOUT = 2 * (N_PY // 2) + len(LONE) - 1
PARTS = ((0, 3), (3, 3), (6, 3), (9, 3))
Z, XU, XD, FU, FD, ZU, ZD, ZF = 0, 4, 5, 6, 7, 8, 12, 16


def iota(shape, dim):
    return lax.broadcasted_iota(jnp.int32, shape, dim)


def ones_where(mask):
    return jnp.where(mask, 1.0, 0.0).astype(BF16)


def dot(a, b):
    return jnp.dot(a, b, preferred_element_type=F32)


def fill_packers(py, sbd):
    p, n = iota((TILE, 128), 0), iota((TILE, 128), 1)
    i, m = n % 16, (n // 16 - py) & 7
    hit = p == RB * i + jnp.where(m >= 4, RB - 1, 0)
    for k in range(4):
        sbd[k] = ones_where(hit & ((m & 3) == k))


def fill_selectors(px, py, sring, sedge, scorner, sconv):
    row, m = iota((128, 128), 0), iota((128, 128), 1)
    i, j = row % 32, row // 32
    i16, item = row % 16, (row // 16 - py) & 7
    here, left, right = (j - px) & 3, (j - px + 1) & 3, (j - px - 1) & 3
    aims = (
        (here, TOP + 1 + i),
        (here, BOTTOM + 1 + i),
        (item & 3, jnp.where(item >= 4, LEFT + i16, -1)),
        (item & 3, jnp.where(item < 4, RIGHT + i16, -1)),
        (left, jnp.where(i == 31, TOP, -1)),
        (right, jnp.where(i == 0, TOP + 33, -1)),
        (left, jnp.where(i == 31, BOTTOM, -1)),
        (right, jnp.where(i == 0, BOTTOM + 33, -1)),
    )
    for slot, (k, aim) in enumerate(aims):
        for face in range(4):
            sring[128 * slot : 128 * slot + 128, 128 * face : 128 * face + 128] = ones_where(
                (k == face) & (m == aim)
            )
    none = jnp.full((128, 128), -1000, jnp.int32)
    for edge in range(4):
        if edge < 2:
            base = (TOP, BOTTOM)[edge]
            at = jnp.where((m >= base) & (m < base + 34), RB * px - 1 + m - base, none)
        else:
            base, shift = (LEFT, RIGHT)[edge - 2], 33 * (edge - 2)
            at = jnp.where((m >= base) & (m < base + 16), RA * py + m - base, none)
            at = jnp.where(m == TOP + shift, RA * py - 1, at)
            at = jnp.where(m == BOTTOM + shift, RA * py + RA, at)
        sedge[edge, :, 0:128] = ones_where(row == at)
        sedge[edge, :, 128:256] = ones_where(row == SIDE - 1 - at)
        cell = m == (TOP, TOP + 33, BOTTOM, BOTTOM + 33)[edge]
        scorner[edge, :, 0:128] = ones_where(cell & (row == 0))
        scorner[edge, :, 128:256] = ones_where(cell & (row == SIDE - 1))
    lane, p = iota((128, TILE), 0), iota((128, TILE), 1)
    for tap in range(9):
        pa, pb = p // RB + tap // 3, p % RB + tap % 3
        cell = jnp.where(
            pa == 0,
            TOP + pb,
            jnp.where(
                pa == RA + 1,
                BOTTOM + pb,
                jnp.where(pb == 0, LEFT + pa - 1, jnp.where(pb == RB + 1, RIGHT + pa - 1, -1)),
            ),
        )
        sconv[128 * tap : 128 * tap + 128, :] = ones_where(lane == cell)


def kernel(
    edge_ref,
    corner_ref,
    feat_ref,
    cot_hbm,
    w_hbm,
    act_hbm,
    grad_hbm,
    held,
    act_ref,
    grad_ref,
    cot_ref,
    w_ref,
    bd,
    bdc,
    hal,
    linr,
    linc,
    full,
    ring,
    pre,
    ringy,
    extra,
    wst,
    sbd,
    sring,
    sedge,
    scorner,
    sconv,
    load_sem,
    ag_send,
    ag_recv,
    rg_send,
    rg_recv,
    halo_send,
    halo_recv,
    line_send,
    line_recv,
    pair_send,
    pair_recv,
):
    px, py, ch = lax.axis_index("px"), lax.axis_index("py"), lax.axis_index("ch")
    z, x = ch // N_X, ch % N_X
    up_x = z * N_X + (x + 1) % N_X
    down_x = z * N_X + (x + N_X - 1) % N_X
    far = (1 - z) * N_X + x
    opp_x = z * N_X + (x + 2) % N_X
    far_up = (1 - z) * N_X + (x + 1) % N_X
    far_down = (1 - z) * N_X + (x + N_X - 1) % N_X
    sides = (py == 0, py == N_PY - 1, px == 0, px == N_PX - 1)
    border = sides[0] | sides[1] | sides[2] | sides[3]
    at_row, at_col = sides[0] | sides[1], sides[2] | sides[3]
    odd = py % 2

    def rows(c):
        return pl.ds(pl.multiple_of(CB * c, CB), CB)

    loads = (
        pltpu.make_async_copy(feat_ref, held.at[0, :, rows(ch), pl.ds(0, TILE)], load_sem.at[0]),
        pltpu.make_async_copy(w_hbm, w_ref, load_sem.at[1]),
        pltpu.make_async_copy(cot_hbm, cot_ref, load_sem.at[2]),
    )
    for load in loads:
        load.start()
    keep_act = pltpu.make_async_copy(act_ref, act_hbm, load_sem.at[3])

    def keep_grad(g):
        part = pl.ds(pl.multiple_of(4 * g, 4), 4)
        return pltpu.make_async_copy(grad_ref.at[part], grad_hbm.at[part], load_sem.at[4 + g])

    barrier = pltpu.get_barrier_semaphore()

    def greet(t, carry):
        tx, ty = t // N_PY, t % N_PY

        @pl.when((tx != px) | (ty != py))
        def _():
            pl.semaphore_signal(barrier, inc=1, device_id={"px": tx, "py": ty}, device_id_type=MESH)

        return carry

    lax.fori_loop(0, N_PX * N_PY, greet, 0)
    for peer in (far, up_x, down_x, opp_x):
        pl.semaphore_signal(barrier, inc=1, device_id={"ch": peer}, device_id_type=MESH)

    def pack_rows(s, lanes, turn):
        lane = iota((3 * CB, 128), 1)
        packed = None
        for k in range(4):
            part = jnp.concatenate(
                [held[s, 4 * q + k, rows(ch), lanes : lanes + 128] for q in range(3)], axis=0
            ).astype(F32)
            shift = (32 * (k + turn)) % 128
            if shift:
                part = pltpu.roll(part, shift, 1)
            packed = part if packed is None else jnp.where(lane // 32 == k, part, packed)
        return pltpu.roll(packed, 32 * px, 1).astype(BF16)

    def pack(s):
        packed = None
        for k in range(4):
            part = jnp.concatenate(
                [held[s, 4 * q + k, rows(ch), 0:TILE] for q in range(3)], axis=0
            )
            term = dot(part, sbd[k])
            packed = term if packed is None else packed + term
        cols = packed
        bd[s, 0] = pack_rows(s, 0, 0)
        bd[s, 1] = pack_rows(s, TILE - 128, 1)
        bd[s, 2] = cols.astype(BF16)
        first = (((iota((CB, 128), 1) // 16 - py) & 7) < 4) == (px == 0)
        folded = jnp.where(first, cols[0:CB], pltpu.roll(cols[CB : 2 * CB], 64, 1))
        bdc[s, 0:CB, :] = folded.astype(BF16)
        bdc[s, CB : 2 * CB, :] = cols[2 * CB : 3 * CB].astype(BF16)

    fill_packers(py, sbd)
    loads[0].wait()
    pack(0)
    fill_selectors(px, py, sring, sedge, scorner, sconv)
    loads[1].wait()
    pick_row = ones_where(iota((CB, 128), 1) == CB * ch + iota((CB, 128), 0))
    for tap in range(9):
        wst[0, CB * tap : CB * tap + CB, :] = w_ref[tap, rows(ch), :]
        wst[1, CB * tap : CB * tap + CB, :] = lax.dot_general(
            pick_row, w_ref[8 - tap], (((1,), (1,)), ((), ())), preferred_element_type=F32
        ).astype(BF16)
    for s in range(2):
        for dx, dy, kind, slot in HALO:
            sx, sy = px - dx, py - dy

            @pl.when((sx < 0) | (sx >= N_PX) | (sy < 0) | (sy >= N_PY))
            def _():
                hal[s, slot] = jnp.zeros((3 * CB, 128), BF16)

    loads[2].wait()
    pl.semaphore_wait(barrier, N_PX * N_PY - 1 + 4)

    def remote(ref, send, recv, device, dst=None):
        return pltpu.make_async_remote_copy(
            src_ref=ref,
            dst_ref=ref if dst is None else dst,
            send_sem=send,
            recv_sem=recv,
            device_id=device,
            device_id_type=MESH,
        )

    def ag_copy(s, index):
        if index < XU:
            block, target, (first, count) = ch, far, PARTS[index]
        elif index < ZU:
            block, target, first, count = (
                (ch, up_x, 0, FACES),
                (ch, down_x, 0, FACES),
                (down_x, up_x, 0, FACES // 2),
                (up_x, down_x, FACES // 2, FACES // 2),
            )[index - XU]
        elif index < ZF:
            part = (index - ZU) % 4
            block, target, (first, count) = far, up_x if index < ZD else down_x, PARTS[part]
        else:
            part = index - ZF
            block, target = ((far_down, up_x), (far_up, down_x), (far, opp_x), (far, opp_x))[part]
            first, count = PARTS[part]
        ref = held.at[s, pl.ds(first, count), rows(block), pl.ds(0, TILE)]
        return remote(ref, ag_send.at[s, index], ag_recv.at[s, index], {"ch": target})

    def rg_copy(s, index):
        block, target, first, count = (
            (ch, far, 0, 12),
            (ch, up_x, 0, 12),
            (ch, down_x, 0, 12),
            (far, up_x, 0, 12),
            (far, down_x, 0, 12),
            (ch, opp_x, 0, 12),
            (far, opp_x, 0, 12),
        )[index]
        ref = held.at[s, pl.ds(first, count), rows(block), pl.ds(TILE, RING)]
        return remote(ref, rg_send.at[s, index], rg_recv.at[s, index], {"ch": target})

    def halo_copy(s, n):
        dx, dy, kind, slot = HALO[n]
        return remote(
            bd.at[s, kind],
            halo_send.at[s, slot],
            halo_recv.at[s, slot],
            {"px": px + dx, "py": py + dy},
            hal.at[s, slot],
        )

    def inside(qx, qy):
        return (qx >= 0) & (qx < N_PX) & (qy >= 0) & (qy < N_PY)

    row_kind = py // (N_PY - 1)
    row_slot = N_PX * row_kind + px
    col_slot = N_PY * odd + (N_PY // 2) * (px // (N_PX - 1)) + py // 2
    here = {"px": px, "py": py}

    def line_copy(s, cols, device):
        if cols:
            return remote(
                bdc.at[s],
                line_send.at[s, 1],
                line_recv.at[s, 1],
                device,
                linc.at[s, col_slot],
            )
        return remote(
            bd.at[s, row_kind],
            line_send.at[s, 0],
            line_recv.at[s, 0],
            device,
            linr.at[s, row_slot],
        )

    def many_lines(s, cols, count):
        ref = (linc if cols else linr).at[s, pl.ds(0, count)]
        return remote(ref, line_send.at[s, cols], line_recv.at[s, cols], here)

    def pair_copy(s, cols):
        if cols:
            ref = linc.at[s, pl.ds(pl.multiple_of(N_PY * odd, N_PY), N_PY)]
        else:
            ref = linr.at[s, pl.ds(pl.multiple_of(N_PX * odd, N_PX), N_PX)]
        return remote(
            ref, pair_send.at[s, cols], pair_recv.at[s, cols], {"py": py + 1 - 2 * odd}
        )

    def send_lines(s):
        for cols in range(2):

            @pl.when((at_row, at_col)[cols])
            def _():
                for tx in (0, N_PX - 1):
                    for j in range(N_PY // 2):
                        ty = 2 * j + odd

                        @pl.when((px != tx) | (py != ty))
                        def _():
                            line_copy(s, cols, {"px": tx, "py": ty}).start()

                for tx, ty in LONE:

                    @pl.when((px != tx) | (py != ty))
                    def _():
                        line_copy(s, cols, {"px": tx, "py": ty}).start()

                if cols:
                    linc[s, col_slot] = bdc[s]
                else:
                    linr[s, row_slot] = bd[s, row_kind]

    def take_lines(s):
        @pl.when(at_col)
        def _():
            @pl.when(at_row)
            def _():
                many_lines(s, 0, N_PX - 1).wait_recv()

            @pl.when(jnp.logical_not(at_row))
            def _():
                many_lines(s, 0, N_PX).wait_recv()

            pair_copy(s, 0).start()
            many_lines(s, 1, N_PY - 1).wait_recv()
            pair_copy(s, 1).start()
            for cols in range(2):
                pair_copy(s, cols).wait_recv()

        @pl.when(at_row & jnp.logical_not(at_col))
        def _():
            many_lines(s, 0, 2 * N_PX - 1).wait_recv()
            many_lines(s, 1, 2 * N_PY).wait_recv()

    def make_ring(s):
        cells = jnp.concatenate([hal[s, slot] for slot in range(8)], axis=1)
        inner = dot(cells, sring[...])
        for q in range(3):
            for k in range(4):
                ring[4 * q + k] = inner[CB * q : CB * q + CB, 128 * k : 128 * k + 128]

        @pl.when(border)
        def _():
            lane = iota((3 * CB, 128), 1)
            for side in range(2):
                parts = [linr[s, N_PX * side + j].astype(F32) for j in range(N_PX)]
                for k in range(4):
                    line = parts[0]
                    for j in range(1, N_PX):
                        line = jnp.where(lane // 32 == (k + j) % 4, parts[j], line)
                    if k:
                        line = pltpu.roll(line, 128 - 32 * k, 1)
                    line = line.astype(BF16)
                    for q in range(3):
                        full[12 * side + 4 * q + k] = line[CB * q : CB * q + CB, :]
            lane = iota((2 * CB, 128), 1)
            for last in range(2):
                parts = [
                    linc[s, N_PY * (j % 2) + (N_PY // 2) * last + j // 2].astype(F32)
                    for j in range(N_PY)
                ]
                for m in range(8):
                    line = parts[0]
                    for j in range(1, N_PY):
                        line = jnp.where(lane // 16 == (m + j) % 8, parts[j], line)
                    if m:
                        line = pltpu.roll(line, 128 - 16 * m, 1)
                    line = line.astype(BF16)
                    face = (m + 4 * last) % 8
                    full[12 * (2 + last) + face] = line[0:CB, :]
                    if face < 4:
                        full[12 * (2 + last) + 8 + face] = line[CB : 2 * CB, :]
            for edge in range(4):

                @pl.when(sides[edge])
                def _():
                    found = jnp.concatenate(
                        [full[12 * edge_ref[1, edge, f] + edge_ref[0, edge, f]] for f in range(FACES)],
                        axis=0,
                    )
                    both = dot(found, sedge[edge])
                    for f in range(FACES):
                        mine = both[CB * f : CB * f + CB]
                        ring[f] += jnp.where(
                            edge_ref[2, edge, f] == 1, mine[:, 128:256], mine[:, 0:128]
                        )

            for corner in range(4):

                @pl.when(sides[corner // 2] & sides[2 + corner % 2])
                def _():
                    found = jnp.concatenate(
                        [
                            full[12 * (corner_ref[corner, 1, f] // 2) + corner_ref[corner, 0, f]]
                            for f in range(FACES)
                        ],
                        axis=0,
                    )
                    both = dot(found, scorner[corner])
                    for f in range(FACES):
                        mine = both[CB * f : CB * f + CB]
                        ring[f] += jnp.where(
                            corner_ref[corner, 1, f] % 2 == 1, mine[:, 128:256], mine[:, 0:128]
                        )

        held[s, :, rows(ch), TILE:WIDE] = ring[...].astype(BF16)

    p = iota((CB, TILE), 1)
    a, b = p // RB, p % RB
    keep_a = (a >= 1, None, a < RA - 1)
    keep_b = (b >= 1, None, b < RB - 1)

    def inner_conv(s, part):
        for f in range(PARTS[part][0], sum(PARTS[part])):
            y = dot(wst[s], held[s, f, :, 0:TILE])
            total = None
            for dj in range(3):
                column = None
                for di in range(3):
                    tap = 3 * di + dj
                    term = y[CB * tap : CB * tap + CB]
                    if di != 1:
                        term = pltpu.roll(term, (-(di - 1) * RB) % TILE, 1)
                        term = jnp.where(keep_a[di], term, 0.0)
                    column = term if column is None else column + term
                if dj != 1:
                    column = pltpu.roll(column, (-(dj - 1)) % TILE, 1)
                    column = jnp.where(keep_b[dj], column, 0.0)
                total = column if total is None else total + column
            pre[f] = total

    def ring_conv(s):
        for f in range(FACES):
            y = dot(wst[s], held[s, f, :, TILE:WIDE])
            edge = jnp.concatenate([y[CB * tap : CB * tap + CB] for tap in range(9)], axis=1)
            high = edge.astype(BF16)
            ringy[f, 0:CB, :] = high
            ringy[f, CB : 2 * CB, :] = (edge - high.astype(F32)).astype(BF16)

        cells = ringy[...].reshape(2 * CB * FACES, 9 * RING)
        extra[...] = dot(cells, sconv[...]).reshape(FACES, 2, CB, TILE)

        def add_ring(g, carry):
            first = pl.multiple_of(4 * g, 4)
            more = extra[pl.ds(first, 4)]
            v = pre[pl.ds(first, 4)] + more[:, 0] + more[:, 1]
            if s == 0:
                sig = 1.0 / (1.0 + jnp.exp(-v))
                act_ref[pl.ds(first, 4)] = (v * sig).astype(BF16)
                slope = cot_ref[pl.ds(first, 4)].astype(F32) * sig * (1.0 + v * (1.0 - sig))
                held[1, pl.ds(first, 4), rows(ch), 0:TILE] = slope.astype(BF16)
            else:
                grad_ref[pl.ds(first, 4)] = v.astype(BF16)
                keep_grad(g).start()
            return carry

        lax.fori_loop(0, FACES // 4, add_ring, 0)
        if s == 0:
            keep_act.start()

    for s in range(2):
        if s == 1:
            pack(1)
        for n, (dx, dy, kind, slot) in enumerate(HALO):

            @pl.when(inside(px + dx, py + dy))
            def _():
                halo_copy(s, n).start()

        send_lines(s)
        for index in (Z, XU, XD, Z + 1, Z + 2, Z + 3):
            ag_copy(s, index).start()

        def sent(*indices):
            for index in indices:
                ag_copy(s, index).wait_send()

        def came(*indices):
            for index in indices:
                ag_copy(s, index).wait_recv()

        def go(*indices):
            for index in indices:
                ag_copy(s, index).start()

        def ring_came(*indices):
            for index in indices:
                rg_copy(s, index).wait_recv()

        def ring_go(*indices):
            for index in indices:
                rg_copy(s, index).start()

        came(XU, XD)
        go(FU, FD)
        came(Z)
        go(ZU, ZD)
        came(Z + 1)
        go(ZU + 1, ZD + 1)
        for n, (dx, dy, kind, slot) in enumerate(HALO):

            @pl.when(inside(px - dx, py - dy))
            def _():
                halo_copy(s, n).wait_recv()

        take_lines(s)
        make_ring(s)
        ring_go(0, 1, 2, 5)
        came(Z + 2)
        go(ZU + 2, ZD + 2, ZF + 2)
        came(ZU)
        go(ZF)
        came(ZD + 1)
        go(ZF + 1)
        came(Z + 3)
        go(ZU + 3, ZD + 3, ZF + 3)
        ring_came(0)
        ring_go(3, 4, 6)
        came(FU, FD, ZD, ZF)
        inner_conv(s, 0)
        came(ZU + 1, ZF + 1)
        inner_conv(s, 1)
        came(ZU + 2, ZD + 2, ZF + 2)
        inner_conv(s, 2)
        came(ZU + 3, ZD + 3, ZF + 3)
        inner_conv(s, 3)
        ring_came(1, 2, 3, 4, 5, 6)
        ring_conv(s)

    for s in range(2):
        for index in range(Z, ZF + 4):
            ag_copy(s, index).wait_send()
        for index in range(7):
            rg_copy(s, index).wait_send()
        for n, (dx, dy, kind, slot) in enumerate(HALO):

            @pl.when(inside(px + dx, py + dy))
            def _():
                halo_copy(s, n).wait_send()

        for cols in range(2):

            @pl.when((at_row, at_col)[cols])
            def _():
                many_lines(s, cols, FANOUT).wait_send()

            @pl.when(at_col)
            def _():
                pair_copy(s, cols).wait_send()

    keep_act.wait()
    for g in range(FACES // 4):
        keep_grad(g).wait()


def local(features, cotangent, weight, edge_table, corner_table):
    def by_face(v):
        return jnp.transpose(v.reshape(CB, FACES, TILE), (1, 0, 2))

    smem = pl.BlockSpec(memory_space=pltpu.SMEM)
    hbm = pl.BlockSpec(memory_space=pl.ANY)
    field = jax.ShapeDtypeStruct((FACES, CB, TILE), BF16)
    act, grad = pl.pallas_call(
        kernel,
        out_shape=(field, field),
        in_specs=[smem, smem, hbm, hbm, hbm],
        out_specs=(hbm, hbm),
        scratch_shapes=[
            pltpu.VMEM((2, FACES, 8 * CB, WIDE), BF16),
            pltpu.VMEM((FACES, CB, TILE), BF16),
            pltpu.VMEM((FACES, CB, TILE), BF16),
            pltpu.VMEM((FACES, CB, TILE), BF16),
            pltpu.VMEM((9, 8 * CB, 8 * CB), BF16),
            pltpu.VMEM((2, 3, 3 * CB, 128), BF16),
            pltpu.VMEM((2, 2 * CB, 128), BF16),
            pltpu.VMEM((2, 8, 3 * CB, 128), BF16),
            pltpu.VMEM((2, FANOUT, 3 * CB, 128), BF16),
            pltpu.VMEM((2, 2 * N_PY, 2 * CB, 128), BF16),
            pltpu.VMEM((48, CB, 128), BF16),
            pltpu.VMEM((FACES, CB, RING), F32),
            pltpu.VMEM((FACES, CB, TILE), F32),
            pltpu.VMEM((FACES, 2 * CB, 9 * RING), BF16),
            pltpu.VMEM((FACES, 2, CB, TILE), F32),
            pltpu.VMEM((2, 9 * CB, 128), BF16),
            pltpu.VMEM((4, TILE, 128), BF16),
            pltpu.VMEM((1024, 512), BF16),
            pltpu.VMEM((4, 128, 256), BF16),
            pltpu.VMEM((4, 128, 256), BF16),
            pltpu.VMEM((9 * RING, TILE), BF16),
            pltpu.SemaphoreType.DMA((7,)),
            pltpu.SemaphoreType.DMA((2, ZF + 4)),
            pltpu.SemaphoreType.DMA((2, ZF + 4)),
            pltpu.SemaphoreType.DMA((2, 9)),
            pltpu.SemaphoreType.DMA((2, 9)),
            pltpu.SemaphoreType.DMA((2, 8)),
            pltpu.SemaphoreType.DMA((2, 8)),
            pltpu.SemaphoreType.DMA((2, 2)),
            pltpu.SemaphoreType.DMA((2, 2)),
            pltpu.SemaphoreType.DMA((2, 2)),
            pltpu.SemaphoreType.DMA((2, 2)),
        ],
        compiler_params=pltpu.CompilerParams(
            collective_id=0, has_side_effects=True, vmem_limit_bytes=56 * 1024 * 1024
        ),
        name="conv_pair",
    )(
        jnp.transpose(edge_table, (2, 1, 0)),
        jnp.transpose(corner_table, (1, 2, 0)),
        by_face(features),
        by_face(cotangent),
        weight.reshape(9, 8 * CB, 8 * CB),
    )

    def by_channel(v):
        return jnp.transpose(v, (1, 0, 2)).reshape(CB, FACES, 1, 1, TILE)

    return by_channel(act), by_channel(grad)


def solution(mesh):
    field = P("ch", None, "py", "px", None)
    return jax.shard_map(
        local,
        mesh=mesh,
        in_specs=(field, field, P(), P(), P()),
        out_specs=(field, field),
        check_vma=False,
    )
```

```python
import functools

import jax
import jax.numpy as jnp
from jax import lax
from jax.experimental import pallas as pl
from jax.experimental.pallas import tpu as pltpu
from jax.sharding import PartitionSpec as P

MESH = pl.DeviceIdType.MESH
F32 = jnp.float32
BF16 = jnp.bfloat16
FACES, CB, RA, RB, TILE = 12, 16, 16, 32, 512
N_PX, N_PY, N_X, N_Z = 4, 8, 4, 2
SIDE = 128
RING = 128
WIDE = TILE + RING

TOP, BOTTOM, LEFT, RIGHT = 0, 34, 68, 84
HALO = (
    (0, 1, 1, 0),
    (0, -1, 0, 1),
    (1, 0, 2, 2),
    (-1, 0, 2, 3),
    (1, 1, 1, 4),
    (-1, 1, 1, 5),
    (1, -1, 0, 6),
    (-1, -1, 0, 7),
)
LONE = ((1, 0), (2, 0), (1, N_PY - 1), (2, N_PY - 1))
FANOUT = 2 * (N_PY // 2) + len(LONE) - 1
PARTS = ((0, 3), (3, 3), (6, 3), (9, 3))
Z, XU, XD, FU, FD, ZU, ZD, ZF = 0, 4, 5, 6, 7, 8, 12, 16


def iota(shape, dim):
    return lax.broadcasted_iota(jnp.int32, shape, dim)


def ones_where(mask):
    return jnp.where(mask, 1.0, 0.0).astype(BF16)


def dot(a, b):
    return jnp.dot(a, b, preferred_element_type=F32)


def fill_packers(py, sbd):
    p, n = iota((TILE, 128), 0), iota((TILE, 128), 1)
    i, m = n % 16, (n // 16 - py) & 7
    hit = p == RB * i + jnp.where(m >= 4, RB - 1, 0)
    for k in range(4):
        sbd[k] = ones_where(hit & ((m & 3) == k))


def fill_selectors(px, py, sring, sedge, scorner, sconv):
    row, m = iota((128, 128), 0), iota((128, 128), 1)
    i, j = row % 32, row // 32
    i16, item = row % 16, (row // 16 - py) & 7
    here, left, right = (j - px) & 3, (j - px + 1) & 3, (j - px - 1) & 3
    aims = (
        (here, TOP + 1 + i),
        (here, BOTTOM + 1 + i),
        (item & 3, jnp.where(item >= 4, LEFT + i16, -1)),
        (item & 3, jnp.where(item < 4, RIGHT + i16, -1)),
        (left, jnp.where(i == 31, TOP, -1)),
        (right, jnp.where(i == 0, TOP + 33, -1)),
        (left, jnp.where(i == 31, BOTTOM, -1)),
        (right, jnp.where(i == 0, BOTTOM + 33, -1)),
    )
    for slot, (k, aim) in enumerate(aims):
        for face in range(4):
            sring[128 * slot : 128 * slot + 128, 128 * face : 128 * face + 128] = ones_where(
                (k == face) & (m == aim)
            )
    none = jnp.full((128, 128), -1000, jnp.int32)
    for edge in range(4):
        if edge < 2:
            base = (TOP, BOTTOM)[edge]
            at = jnp.where((m >= base) & (m < base + 34), RB * px - 1 + m - base, none)
        else:
            base, shift = (LEFT, RIGHT)[edge - 2], 33 * (edge - 2)
            at = jnp.where((m >= base) & (m < base + 16), RA * py + m - base, none)
            at = jnp.where(m == TOP + shift, RA * py - 1, at)
            at = jnp.where(m == BOTTOM + shift, RA * py + RA, at)
        sedge[edge, :, 0:128] = ones_where(row == at)
        sedge[edge, :, 128:256] = ones_where(row == SIDE - 1 - at)
        cell = m == (TOP, TOP + 33, BOTTOM, BOTTOM + 33)[edge]
        scorner[edge, :, 0:128] = ones_where(cell & (row == 0))
        scorner[edge, :, 128:256] = ones_where(cell & (row == SIDE - 1))
    lane, p = iota((128, TILE), 0), iota((128, TILE), 1)
    for tap in range(9):
        pa, pb = p // RB + tap // 3, p % RB + tap % 3
        cell = jnp.where(
            pa == 0,
            TOP + pb,
            jnp.where(
                pa == RA + 1,
                BOTTOM + pb,
                jnp.where(pb == 0, LEFT + pa - 1, jnp.where(pb == RB + 1, RIGHT + pa - 1, -1)),
            ),
        )
        sconv[128 * tap : 128 * tap + 128, :] = ones_where(lane == cell)


def kernel(
    edge_ref,
    corner_ref,
    feat_ref,
    cot_hbm,
    w_hbm,
    act_ref,
    grad_ref,
    held,
    cot_ref,
    w_ref,
    bd,
    bdc,
    hal,
    linr,
    linc,
    full,
    ring,
    pre,
    ringy,
    extra,
    wst,
    sbd,
    sring,
    sedge,
    scorner,
    sconv,
    load_sem,
    ag_send,
    ag_recv,
    rg_send,
    rg_recv,
    halo_send,
    halo_recv,
    line_send,
    line_recv,
    pair_send,
    pair_recv,
):
    px, py, ch = lax.axis_index("px"), lax.axis_index("py"), lax.axis_index("ch")
    z, x = ch // N_X, ch % N_X
    up_x = z * N_X + (x + 1) % N_X
    down_x = z * N_X + (x + N_X - 1) % N_X
    far = (1 - z) * N_X + x
    opp_x = z * N_X + (x + 2) % N_X
    far_up = (1 - z) * N_X + (x + 1) % N_X
    far_down = (1 - z) * N_X + (x + N_X - 1) % N_X
    sides = (py == 0, py == N_PY - 1, px == 0, px == N_PX - 1)
    border = sides[0] | sides[1] | sides[2] | sides[3]
    at_row, at_col = sides[0] | sides[1], sides[2] | sides[3]
    odd = py % 2

    def rows(c):
        return pl.ds(pl.multiple_of(CB * c, CB), CB)

    loads = (
        pltpu.make_async_copy(feat_ref, held.at[0, :, rows(ch), pl.ds(0, TILE)], load_sem.at[0]),
        pltpu.make_async_copy(w_hbm, w_ref, load_sem.at[1]),
        pltpu.make_async_copy(cot_hbm, cot_ref, load_sem.at[2]),
    )
    for load in loads:
        load.start()
    barrier = pltpu.get_barrier_semaphore()

    def greet(t, carry):
        tx, ty = t // N_PY, t % N_PY

        @pl.when((tx != px) | (ty != py))
        def _():
            pl.semaphore_signal(barrier, inc=1, device_id={"px": tx, "py": ty}, device_id_type=MESH)

        return carry

    lax.fori_loop(0, N_PX * N_PY, greet, 0)
    for peer in (far, up_x, down_x, opp_x):
        pl.semaphore_signal(barrier, inc=1, device_id={"ch": peer}, device_id_type=MESH)

    def pack_rows(s, lanes, turn):
        lane = iota((3 * CB, 128), 1)
        packed = None
        for k in range(4):
            part = jnp.concatenate(
                [held[s, 4 * q + k, rows(ch), lanes : lanes + 128] for q in range(3)], axis=0
            ).astype(F32)
            shift = (32 * (k + turn)) % 128
            if shift:
                part = pltpu.roll(part, shift, 1)
            packed = part if packed is None else jnp.where(lane // 32 == k, part, packed)
        return pltpu.roll(packed, 32 * px, 1).astype(BF16)

    def pack(s):
        packed = None
        for k in range(4):
            part = jnp.concatenate(
                [held[s, 4 * q + k, rows(ch), 0:TILE] for q in range(3)], axis=0
            )
            term = dot(part, sbd[k])
            packed = term if packed is None else packed + term
        cols = packed
        bd[s, 0] = pack_rows(s, 0, 0)
        bd[s, 1] = pack_rows(s, TILE - 128, 1)
        bd[s, 2] = cols.astype(BF16)
        first = (((iota((CB, 128), 1) // 16 - py) & 7) < 4) == (px == 0)
        folded = jnp.where(first, cols[0:CB], pltpu.roll(cols[CB : 2 * CB], 64, 1))
        bdc[s, 0:CB, :] = folded.astype(BF16)
        bdc[s, CB : 2 * CB, :] = cols[2 * CB : 3 * CB].astype(BF16)

    fill_packers(py, sbd)
    loads[0].wait()
    pack(0)
    fill_selectors(px, py, sring, sedge, scorner, sconv)
    loads[1].wait()
    pick_row = ones_where(iota((CB, 128), 1) == CB * ch + iota((CB, 128), 0))
    for tap in range(9):
        wst[0, CB * tap : CB * tap + CB, :] = w_ref[tap, rows(ch), :]
        wst[1, CB * tap : CB * tap + CB, :] = lax.dot_general(
            pick_row, w_ref[8 - tap], (((1,), (1,)), ((), ())), preferred_element_type=F32
        ).astype(BF16)
    for s in range(2):
        for dx, dy, kind, slot in HALO:
            sx, sy = px - dx, py - dy

            @pl.when((sx < 0) | (sx >= N_PX) | (sy < 0) | (sy >= N_PY))
            def _():
                hal[s, slot] = jnp.zeros((3 * CB, 128), BF16)

    loads[2].wait()
    pl.semaphore_wait(barrier, N_PX * N_PY - 1 + 4)

    def remote(ref, send, recv, device, dst=None):
        return pltpu.make_async_remote_copy(
            src_ref=ref,
            dst_ref=ref if dst is None else dst,
            send_sem=send,
            recv_sem=recv,
            device_id=device,
            device_id_type=MESH,
        )

    def ag_copy(s, index):
        if index < XU:
            block, target, (first, count) = ch, far, PARTS[index]
        elif index < ZU:
            block, target, first, count = (
                (ch, up_x, 0, FACES),
                (ch, down_x, 0, FACES),
                (down_x, up_x, 0, FACES // 2),
                (up_x, down_x, FACES // 2, FACES // 2),
            )[index - XU]
        elif index < ZF:
            part = (index - ZU) % 4
            block, target, (first, count) = far, up_x if index < ZD else down_x, PARTS[part]
        else:
            part = index - ZF
            block, target = ((far_down, up_x), (far_up, down_x), (far, opp_x), (far, opp_x))[part]
            first, count = PARTS[part]
        ref = held.at[s, pl.ds(first, count), rows(block), pl.ds(0, TILE)]
        return remote(ref, ag_send.at[s, index], ag_recv.at[s, index], {"ch": target})

    def rg_copy(s, index):
        block, target, first, count = (
            (ch, far, 0, 12),
            (ch, up_x, 0, 12),
            (ch, down_x, 0, 12),
            (far, up_x, 0, 12),
            (far, down_x, 0, 12),
            (ch, opp_x, 0, 12),
            (far, opp_x, 0, 12),
        )[index]
        ref = held.at[s, pl.ds(first, count), rows(block), pl.ds(TILE, RING)]
        return remote(ref, rg_send.at[s, index], rg_recv.at[s, index], {"ch": target})

    def halo_copy(s, n):
        dx, dy, kind, slot = HALO[n]
        return remote(
            bd.at[s, kind],
            halo_send.at[s, slot],
            halo_recv.at[s, slot],
            {"px": px + dx, "py": py + dy},
            hal.at[s, slot],
        )

    def inside(qx, qy):
        return (qx >= 0) & (qx < N_PX) & (qy >= 0) & (qy < N_PY)

    row_kind = py // (N_PY - 1)
    row_slot = N_PX * row_kind + px
    col_slot = N_PY * odd + (N_PY // 2) * (px // (N_PX - 1)) + py // 2
    here = {"px": px, "py": py}

    def line_copy(s, cols, device):
        if cols:
            return remote(
                bdc.at[s],
                line_send.at[s, 1],
                line_recv.at[s, 1],
                device,
                linc.at[s, col_slot],
            )
        return remote(
            bd.at[s, row_kind],
            line_send.at[s, 0],
            line_recv.at[s, 0],
            device,
            linr.at[s, row_slot],
        )

    def many_lines(s, cols, count):
        ref = (linc if cols else linr).at[s, pl.ds(0, count)]
        return remote(ref, line_send.at[s, cols], line_recv.at[s, cols], here)

    def pair_copy(s, cols):
        if cols:
            ref = linc.at[s, pl.ds(pl.multiple_of(N_PY * odd, N_PY), N_PY)]
        else:
            ref = linr.at[s, pl.ds(pl.multiple_of(N_PX * odd, N_PX), N_PX)]
        return remote(
            ref, pair_send.at[s, cols], pair_recv.at[s, cols], {"py": py + 1 - 2 * odd}
        )

    def send_lines(s):
        for cols in range(2):

            @pl.when((at_row, at_col)[cols])
            def _():
                for tx in (0, N_PX - 1):
                    for j in range(N_PY // 2):
                        ty = 2 * j + odd

                        @pl.when((px != tx) | (py != ty))
                        def _():
                            line_copy(s, cols, {"px": tx, "py": ty}).start()

                for tx, ty in LONE:

                    @pl.when((px != tx) | (py != ty))
                    def _():
                        line_copy(s, cols, {"px": tx, "py": ty}).start()

                if cols:
                    linc[s, col_slot] = bdc[s]
                else:
                    linr[s, row_slot] = bd[s, row_kind]

    def take_lines(s):
        @pl.when(at_col)
        def _():
            @pl.when(at_row)
            def _():
                many_lines(s, 0, N_PX - 1).wait_recv()

            @pl.when(jnp.logical_not(at_row))
            def _():
                many_lines(s, 0, N_PX).wait_recv()

            pair_copy(s, 0).start()
            many_lines(s, 1, N_PY - 1).wait_recv()
            pair_copy(s, 1).start()
            for cols in range(2):
                pair_copy(s, cols).wait_recv()

        @pl.when(at_row & jnp.logical_not(at_col))
        def _():
            many_lines(s, 0, 2 * N_PX - 1).wait_recv()
            many_lines(s, 1, 2 * N_PY).wait_recv()

    def make_ring(s):
        cells = jnp.concatenate([hal[s, slot] for slot in range(8)], axis=1)
        inner = dot(cells, sring[...])
        for q in range(3):
            for k in range(4):
                ring[4 * q + k] = inner[CB * q : CB * q + CB, 128 * k : 128 * k + 128]

        @pl.when(border)
        def _():
            lane = iota((3 * CB, 128), 1)
            for side in range(2):
                parts = [linr[s, N_PX * side + j].astype(F32) for j in range(N_PX)]
                for k in range(4):
                    line = parts[0]
                    for j in range(1, N_PX):
                        line = jnp.where(lane // 32 == (k + j) % 4, parts[j], line)
                    if k:
                        line = pltpu.roll(line, 128 - 32 * k, 1)
                    line = line.astype(BF16)
                    for q in range(3):
                        full[12 * side + 4 * q + k] = line[CB * q : CB * q + CB, :]
            lane = iota((2 * CB, 128), 1)
            for last in range(2):
                parts = [
                    linc[s, N_PY * (j % 2) + (N_PY // 2) * last + j // 2].astype(F32)
                    for j in range(N_PY)
                ]
                for m in range(8):
                    line = parts[0]
                    for j in range(1, N_PY):
                        line = jnp.where(lane // 16 == (m + j) % 8, parts[j], line)
                    if m:
                        line = pltpu.roll(line, 128 - 16 * m, 1)
                    line = line.astype(BF16)
                    face = (m + 4 * last) % 8
                    full[12 * (2 + last) + face] = line[0:CB, :]
                    if face < 4:
                        full[12 * (2 + last) + 8 + face] = line[CB : 2 * CB, :]
            for edge in range(4):

                @pl.when(sides[edge])
                def _():
                    found = jnp.concatenate(
                        [full[12 * edge_ref[1, edge, f] + edge_ref[0, edge, f]] for f in range(FACES)],
                        axis=0,
                    )
                    both = dot(found, sedge[edge])
                    for f in range(FACES):
                        mine = both[CB * f : CB * f + CB]
                        ring[f] += jnp.where(
                            edge_ref[2, edge, f] == 1, mine[:, 128:256], mine[:, 0:128]
                        )

            for corner in range(4):

                @pl.when(sides[corner // 2] & sides[2 + corner % 2])
                def _():
                    found = jnp.concatenate(
                        [
                            full[12 * (corner_ref[corner, 1, f] // 2) + corner_ref[corner, 0, f]]
                            for f in range(FACES)
                        ],
                        axis=0,
                    )
                    both = dot(found, scorner[corner])
                    for f in range(FACES):
                        mine = both[CB * f : CB * f + CB]
                        ring[f] += jnp.where(
                            corner_ref[corner, 1, f] % 2 == 1, mine[:, 128:256], mine[:, 0:128]
                        )

        held[s, :, rows(ch), TILE:WIDE] = ring[...].astype(BF16)

    p = iota((CB, TILE), 1)
    a, b = p // RB, p % RB
    keep_a = (a >= 1, None, a < RA - 1)
    keep_b = (b >= 1, None, b < RB - 1)

    def inner_conv(s, part):
        for f in range(PARTS[part][0], sum(PARTS[part])):
            y = dot(wst[s], held[s, f, :, 0:TILE])
            total = None
            for dj in range(3):
                column = None
                for di in range(3):
                    tap = 3 * di + dj
                    term = y[CB * tap : CB * tap + CB]
                    if di != 1:
                        term = pltpu.roll(term, (-(di - 1) * RB) % TILE, 1)
                        term = jnp.where(keep_a[di], term, 0.0)
                    column = term if column is None else column + term
                if dj != 1:
                    column = pltpu.roll(column, (-(dj - 1)) % TILE, 1)
                    column = jnp.where(keep_b[dj], column, 0.0)
                total = column if total is None else total + column
            pre[f] = total

    def ring_conv(s):
        for f in range(FACES):
            y = dot(wst[s], held[s, f, :, TILE:WIDE])
            edge = jnp.concatenate([y[CB * tap : CB * tap + CB] for tap in range(9)], axis=1)
            high = edge.astype(BF16)
            ringy[f, 0:CB, :] = high
            ringy[f, CB : 2 * CB, :] = (edge - high.astype(F32)).astype(BF16)

        cells = ringy[...].reshape(2 * CB * FACES, 9 * RING)
        extra[...] = dot(cells, sconv[...]).reshape(FACES, 2, CB, TILE)

        def add_ring(g, carry):
            first = pl.multiple_of(4 * g, 4)
            more = extra[pl.ds(first, 4)]
            v = pre[pl.ds(first, 4)] + more[:, 0] + more[:, 1]
            if s == 0:
                sig = 1.0 / (1.0 + jnp.exp(-v))
                act_ref[pl.ds(first, 4)] = (v * sig).astype(BF16)
                slope = cot_ref[pl.ds(first, 4)].astype(F32) * sig * (1.0 + v * (1.0 - sig))
                held[1, pl.ds(first, 4), rows(ch), 0:TILE] = slope.astype(BF16)
            else:
                grad_ref[pl.ds(first, 4)] = v.astype(BF16)
            return carry

        lax.fori_loop(0, FACES // 4, add_ring, 0)

    for s in range(2):
        if s == 1:
            pack(1)
        for n, (dx, dy, kind, slot) in enumerate(HALO):

            @pl.when(inside(px + dx, py + dy))
            def _():
                halo_copy(s, n).start()

        send_lines(s)
        for index in (Z, XU, XD, Z + 1, Z + 2, Z + 3):
            ag_copy(s, index).start()

        def sent(*indices):
            for index in indices:
                ag_copy(s, index).wait_send()

        def came(*indices):
            for index in indices:
                ag_copy(s, index).wait_recv()

        def go(*indices):
            for index in indices:
                ag_copy(s, index).start()

        def ring_came(*indices):
            for index in indices:
                rg_copy(s, index).wait_recv()

        def ring_go(*indices):
            for index in indices:
                rg_copy(s, index).start()

        came(XU, XD)
        go(FU, FD)
        came(Z)
        go(ZU, ZD)
        came(Z + 1)
        go(ZU + 1, ZD + 1)
        for n, (dx, dy, kind, slot) in enumerate(HALO):

            @pl.when(inside(px - dx, py - dy))
            def _():
                halo_copy(s, n).wait_recv()

        take_lines(s)
        make_ring(s)
        ring_go(0, 1, 2, 5)
        came(Z + 2)
        go(ZU + 2, ZD + 2, ZF + 2)
        came(ZU)
        go(ZF)
        came(ZD + 1)
        go(ZF + 1)
        came(Z + 3)
        go(ZU + 3, ZD + 3, ZF + 3)
        ring_came(0)
        ring_go(3, 4, 6)
        came(FU, FD, ZD, ZF)
        inner_conv(s, 0)
        came(ZU + 1, ZF + 1)
        inner_conv(s, 1)
        came(ZU + 2, ZD + 2, ZF + 2)
        inner_conv(s, 2)
        came(ZU + 3, ZD + 3, ZF + 3)
        inner_conv(s, 3)
        ring_came(1, 2, 3, 4, 5, 6)
        ring_conv(s)

    for s in range(2):
        for index in range(Z, ZF + 4):
            ag_copy(s, index).wait_send()
        for index in range(7):
            rg_copy(s, index).wait_send()
        for n, (dx, dy, kind, slot) in enumerate(HALO):

            @pl.when(inside(px + dx, py + dy))
            def _():
                halo_copy(s, n).wait_send()

        for cols in range(2):

            @pl.when((at_row, at_col)[cols])
            def _():
                many_lines(s, cols, FANOUT).wait_send()

            @pl.when(at_col)
            def _():
                pair_copy(s, cols).wait_send()


def local(features, cotangent, weight, edge_table, corner_table):
    def by_face(v):
        return jnp.transpose(v.reshape(CB, FACES, TILE), (1, 0, 2))

    smem = pl.BlockSpec(memory_space=pltpu.SMEM)
    hbm = pl.BlockSpec(memory_space=pl.ANY)
    field = pltpu.VMEM((FACES, CB, TILE), BF16)
    vmem = pl.BlockSpec(memory_space=pltpu.VMEM)
    act, grad = pl.pallas_call(
        kernel,
        out_shape=(field, field),
        in_specs=[smem, smem, hbm, hbm, hbm],
        out_specs=(vmem, vmem),
        scratch_shapes=[
            pltpu.VMEM((2, FACES, 8 * CB, WIDE), BF16),
            pltpu.VMEM((FACES, CB, TILE), BF16),
            pltpu.VMEM((9, 8 * CB, 8 * CB), BF16),
            pltpu.VMEM((2, 3, 3 * CB, 128), BF16),
            pltpu.VMEM((2, 2 * CB, 128), BF16),
            pltpu.VMEM((2, 8, 3 * CB, 128), BF16),
            pltpu.VMEM((2, FANOUT, 3 * CB, 128), BF16),
            pltpu.VMEM((2, 2 * N_PY, 2 * CB, 128), BF16),
            pltpu.VMEM((48, CB, 128), BF16),
            pltpu.VMEM((FACES, CB, RING), F32),
            pltpu.VMEM((FACES, CB, TILE), F32),
            pltpu.VMEM((FACES, 2 * CB, 9 * RING), BF16),
            pltpu.VMEM((FACES, 2, CB, TILE), F32),
            pltpu.VMEM((2, 9 * CB, 128), BF16),
            pltpu.VMEM((4, TILE, 128), BF16),
            pltpu.VMEM((1024, 512), BF16),
            pltpu.VMEM((4, 128, 256), BF16),
            pltpu.VMEM((4, 128, 256), BF16),
            pltpu.VMEM((9 * RING, TILE), BF16),
            pltpu.SemaphoreType.DMA((3,)),
            pltpu.SemaphoreType.DMA((2, ZF + 4)),
            pltpu.SemaphoreType.DMA((2, ZF + 4)),
            pltpu.SemaphoreType.DMA((2, 9)),
            pltpu.SemaphoreType.DMA((2, 9)),
            pltpu.SemaphoreType.DMA((2, 8)),
            pltpu.SemaphoreType.DMA((2, 8)),
            pltpu.SemaphoreType.DMA((2, 2)),
            pltpu.SemaphoreType.DMA((2, 2)),
            pltpu.SemaphoreType.DMA((2, 2)),
            pltpu.SemaphoreType.DMA((2, 2)),
        ],
        compiler_params=pltpu.CompilerParams(
            collective_id=0, has_side_effects=True, vmem_limit_bytes=56 * 1024 * 1024
        ),
        name="conv_pair",
    )(
        jnp.transpose(edge_table, (2, 1, 0)),
        jnp.transpose(corner_table, (1, 2, 0)),
        by_face(features),
        by_face(cotangent),
        weight.reshape(9, 8 * CB, 8 * CB),
    )

    def by_channel(v):
        return jnp.transpose(v, (1, 0, 2)).reshape(CB, FACES, 1, 1, TILE)

    return by_channel(act), by_channel(grad)


def solution(mesh):
    field = P("ch", None, "py", "px", None)
    return jax.shard_map(
        local,
        mesh=mesh,
        in_specs=(field, field, P(), P(), P()),
        out_specs=(field, field),
        check_vma=False,
    )
```

```python
import functools

import jax
import jax.numpy as jnp
from jax import lax
from jax.experimental import pallas as pl
from jax.experimental.pallas import tpu as pltpu
from jax.sharding import PartitionSpec as P

MESH = pl.DeviceIdType.MESH
F32 = jnp.float32
BF16 = jnp.bfloat16
FACES, CB, RA, RB, TILE = 12, 16, 16, 32, 512
N_PX, N_PY, N_X, N_Z = 4, 8, 4, 2
SIDE = 128
RING = 128
WIDE = TILE + RING

TOP, BOTTOM, LEFT, RIGHT = 0, 34, 68, 84
HALO = (
    (0, 1, 1, 0),
    (0, -1, 0, 1),
    (1, 0, 2, 2),
    (-1, 0, 2, 3),
    (1, 1, 1, 4),
    (-1, 1, 1, 5),
    (1, -1, 0, 6),
    (-1, -1, 0, 7),
)
LONE = ((1, 0), (2, 0), (1, N_PY - 1), (2, N_PY - 1))
FANOUT = 2 * (N_PY // 2) + len(LONE) - 1
PARTS = ((0, 3), (3, 3), (6, 3), (9, 3))
Z, XU, XD, FU, FD, ZU, ZD, ZF = 0, 4, 5, 6, 7, 8, 12, 16


def iota(shape, dim):
    return lax.broadcasted_iota(jnp.int32, shape, dim)


def ones_where(mask):
    return jnp.where(mask, 1.0, 0.0).astype(BF16)


def dot(a, b):
    return jnp.dot(a, b, preferred_element_type=F32)


def fill_packers(py, sbd):
    p, n = iota((TILE, 128), 0), iota((TILE, 128), 1)
    i, m = n % 16, (n // 16 - py) & 7
    hit = p == RB * i + jnp.where(m >= 4, RB - 1, 0)
    for k in range(4):
        sbd[k] = ones_where(hit & ((m & 3) == k))


def fill_selectors(px, py, sring, sedge, scorner, sconv):
    row, m = iota((128, 128), 0), iota((128, 128), 1)
    i, j = row % 32, row // 32
    i16, item = row % 16, (row // 16 - py) & 7
    here, left, right = (j - px) & 3, (j - px + 1) & 3, (j - px - 1) & 3
    aims = (
        (here, TOP + 1 + i),
        (here, BOTTOM + 1 + i),
        (item & 3, jnp.where(item >= 4, LEFT + i16, -1)),
        (item & 3, jnp.where(item < 4, RIGHT + i16, -1)),
        (left, jnp.where(i == 31, TOP, -1)),
        (right, jnp.where(i == 0, TOP + 33, -1)),
        (left, jnp.where(i == 31, BOTTOM, -1)),
        (right, jnp.where(i == 0, BOTTOM + 33, -1)),
    )
    for slot, (k, aim) in enumerate(aims):
        for face in range(4):
            sring[128 * slot : 128 * slot + 128, 128 * face : 128 * face + 128] = ones_where(
                (k == face) & (m == aim)
            )
    none = jnp.full((128, 128), -1000, jnp.int32)
    for edge in range(4):
        if edge < 2:
            base = (TOP, BOTTOM)[edge]
            at = jnp.where((m >= base) & (m < base + 34), RB * px - 1 + m - base, none)
        else:
            base, shift = (LEFT, RIGHT)[edge - 2], 33 * (edge - 2)
            at = jnp.where((m >= base) & (m < base + 16), RA * py + m - base, none)
            at = jnp.where(m == TOP + shift, RA * py - 1, at)
            at = jnp.where(m == BOTTOM + shift, RA * py + RA, at)
        sedge[edge, :, 0:128] = ones_where(row == at)
        sedge[edge, :, 128:256] = ones_where(row == SIDE - 1 - at)
        cell = m == (TOP, TOP + 33, BOTTOM, BOTTOM + 33)[edge]
        scorner[edge, :, 0:128] = ones_where(cell & (row == 0))
        scorner[edge, :, 128:256] = ones_where(cell & (row == SIDE - 1))
    lane, p = iota((128, TILE), 0), iota((128, TILE), 1)
    for tap in range(9):
        pa, pb = p // RB + tap // 3, p % RB + tap % 3
        cell = jnp.where(
            pa == 0,
            TOP + pb,
            jnp.where(
                pa == RA + 1,
                BOTTOM + pb,
                jnp.where(pb == 0, LEFT + pa - 1, jnp.where(pb == RB + 1, RIGHT + pa - 1, -1)),
            ),
        )
        sconv[128 * tap : 128 * tap + 128, :] = ones_where(lane == cell)


def kernel(
    edge_ref,
    corner_ref,
    feat_ref,
    cot_hbm,
    w_hbm,
    act_ref,
    grad_ref,
    held,
    cot_ref,
    w_ref,
    bd,
    bdc,
    hal,
    linr,
    linc,
    full,
    ring,
    pre,
    ringy,
    extra,
    wst,
    sbd,
    sring,
    sedge,
    scorner,
    sconv,
    load_sem,
    ag_send,
    ag_recv,
    rg_send,
    rg_recv,
    halo_send,
    halo_recv,
    line_send,
    line_recv,
    pair_send,
    pair_recv,
):
    px, py, ch = lax.axis_index("px"), lax.axis_index("py"), lax.axis_index("ch")
    z, x = ch // N_X, ch % N_X
    up_x = z * N_X + (x + 1) % N_X
    down_x = z * N_X + (x + N_X - 1) % N_X
    far = (1 - z) * N_X + x
    opp_x = z * N_X + (x + 2) % N_X
    far_up = (1 - z) * N_X + (x + 1) % N_X
    far_down = (1 - z) * N_X + (x + N_X - 1) % N_X
    sides = (py == 0, py == N_PY - 1, px == 0, px == N_PX - 1)
    border = sides[0] | sides[1] | sides[2] | sides[3]
    at_row, at_col = sides[0] | sides[1], sides[2] | sides[3]
    odd = py % 2

    def rows(c):
        return pl.ds(pl.multiple_of(CB * c, CB), CB)

    loads = (
        pltpu.make_async_copy(feat_ref, held.at[0, :, rows(ch), pl.ds(0, TILE)], load_sem.at[0]),
        pltpu.make_async_copy(w_hbm, w_ref, load_sem.at[1]),
        pltpu.make_async_copy(cot_hbm, cot_ref, load_sem.at[2]),
    )
    for load in loads:
        load.start()
    barrier = pltpu.get_barrier_semaphore()

    def greet(t, carry):
        tx, ty = t // N_PY, t % N_PY

        @pl.when((tx != px) | (ty != py))
        def _():
            pl.semaphore_signal(barrier, inc=1, device_id={"px": tx, "py": ty}, device_id_type=MESH)

        return carry

    lax.fori_loop(0, N_PX * N_PY, greet, 0)
    for peer in (far, up_x, down_x, opp_x):
        pl.semaphore_signal(barrier, inc=1, device_id={"ch": peer}, device_id_type=MESH)

    def pack_rows(s, lanes, turn):
        lane = iota((3 * CB, 128), 1)
        packed = None
        for k in range(4):
            part = jnp.concatenate(
                [held[s, 4 * q + k, rows(ch), lanes : lanes + 128] for q in range(3)], axis=0
            ).astype(F32)
            shift = (32 * (k + turn)) % 128
            if shift:
                part = pltpu.roll(part, shift, 1)
            packed = part if packed is None else jnp.where(lane // 32 == k, part, packed)
        return pltpu.roll(packed, 32 * px, 1).astype(BF16)

    def pack(s):
        packed = None
        for k in range(4):
            part = jnp.concatenate(
                [held[s, 4 * q + k, rows(ch), 0:TILE] for q in range(3)], axis=0
            )
            term = dot(part, sbd[k])
            packed = term if packed is None else packed + term
        cols = packed
        bd[s, 0] = pack_rows(s, 0, 0)
        bd[s, 1] = pack_rows(s, TILE - 128, 1)
        bd[s, 2] = cols.astype(BF16)
        first = (((iota((CB, 128), 1) // 16 - py) & 7) < 4) == (px == 0)
        folded = jnp.where(first, cols[0:CB], pltpu.roll(cols[CB : 2 * CB], 64, 1))
        bdc[s, 0:CB, :] = folded.astype(BF16)
        bdc[s, CB : 2 * CB, :] = cols[2 * CB : 3 * CB].astype(BF16)

    fill_packers(py, sbd)
    loads[0].wait()
    pack(0)
    fill_selectors(px, py, sring, sedge, scorner, sconv)
    loads[1].wait()
    pick_row = ones_where(iota((CB, 128), 1) == CB * ch + iota((CB, 128), 0))
    for tap in range(9):
        wst[0, CB * tap : CB * tap + CB, :] = w_ref[tap, rows(ch), :]
        wst[1, CB * tap : CB * tap + CB, :] = lax.dot_general(
            pick_row, w_ref[8 - tap], (((1,), (1,)), ((), ())), preferred_element_type=F32
        ).astype(BF16)
    for s in range(2):
        for dx, dy, kind, slot in HALO:
            sx, sy = px - dx, py - dy

            @pl.when((sx < 0) | (sx >= N_PX) | (sy < 0) | (sy >= N_PY))
            def _():
                hal[s, slot] = jnp.zeros((3 * CB, 128), BF16)

    loads[2].wait()
    pl.semaphore_wait(barrier, N_PX * N_PY - 1 + 4)

    def remote(ref, send, recv, device, dst=None):
        return pltpu.make_async_remote_copy(
            src_ref=ref,
            dst_ref=ref if dst is None else dst,
            send_sem=send,
            recv_sem=recv,
            device_id=device,
            device_id_type=MESH,
        )

    def ag_copy(s, index):
        if index < XU:
            block, target, (first, count) = ch, far, PARTS[index]
        elif index < ZU:
            block, target, first, count = (
                (ch, up_x, 0, FACES),
                (ch, down_x, 0, FACES),
                (down_x, up_x, 0, FACES // 2),
                (up_x, down_x, FACES // 2, FACES // 2),
            )[index - XU]
        elif index < ZF:
            part = (index - ZU) % 4
            block, target, (first, count) = far, up_x if index < ZD else down_x, PARTS[part]
        else:
            part = index - ZF
            block, target = ((far_down, up_x), (far_up, down_x), (far, opp_x), (far, opp_x))[part]
            first, count = PARTS[part]
        ref = held.at[s, pl.ds(first, count), rows(block), pl.ds(0, TILE)]
        return remote(ref, ag_send.at[s, index], ag_recv.at[s, index], {"ch": target})

    def rg_copy(s, index):
        block, target, first, count = (
            (ch, far, 0, 12),
            (ch, up_x, 0, 12),
            (ch, down_x, 0, 12),
            (far, up_x, 0, 12),
            (far, down_x, 0, 12),
            (ch, opp_x, 0, 12),
            (far, opp_x, 0, 12),
        )[index]
        ref = held.at[s, pl.ds(first, count), rows(block), pl.ds(TILE, RING)]
        return remote(ref, rg_send.at[s, index], rg_recv.at[s, index], {"ch": target})

    def halo_copy(s, n):
        dx, dy, kind, slot = HALO[n]
        return remote(
            bd.at[s, kind],
            halo_send.at[s, slot],
            halo_recv.at[s, slot],
            {"px": px + dx, "py": py + dy},
            hal.at[s, slot],
        )

    def inside(qx, qy):
        return (qx >= 0) & (qx < N_PX) & (qy >= 0) & (qy < N_PY)

    row_kind = py // (N_PY - 1)
    row_slot = N_PX * row_kind + px
    col_slot = N_PY * odd + (N_PY // 2) * (px // (N_PX - 1)) + py // 2
    here = {"px": px, "py": py}

    def line_copy(s, cols, device):
        if cols:
            return remote(
                bdc.at[s],
                line_send.at[s, 1],
                line_recv.at[s, 1],
                device,
                linc.at[s, col_slot],
            )
        return remote(
            bd.at[s, row_kind],
            line_send.at[s, 0],
            line_recv.at[s, 0],
            device,
            linr.at[s, row_slot],
        )

    def many_lines(s, cols, count):
        ref = (linc if cols else linr).at[s, pl.ds(0, count)]
        return remote(ref, line_send.at[s, cols], line_recv.at[s, cols], here)

    def pair_copy(s, cols):
        if cols:
            ref = linc.at[s, pl.ds(pl.multiple_of(N_PY * odd, N_PY), N_PY)]
        else:
            ref = linr.at[s, pl.ds(pl.multiple_of(N_PX * odd, N_PX), N_PX)]
        return remote(
            ref, pair_send.at[s, cols], pair_recv.at[s, cols], {"py": py + 1 - 2 * odd}
        )

    def send_lines(s):
        for cols in range(2):

            @pl.when((at_row, at_col)[cols])
            def _():
                for tx in (0, N_PX - 1):
                    for j in range(N_PY // 2):
                        ty = 2 * j + odd

                        @pl.when((px != tx) | (py != ty))
                        def _():
                            line_copy(s, cols, {"px": tx, "py": ty}).start()

                for tx, ty in LONE:

                    @pl.when((px != tx) | (py != ty))
                    def _():
                        line_copy(s, cols, {"px": tx, "py": ty}).start()

                if cols:
                    linc[s, col_slot] = bdc[s]
                else:
                    linr[s, row_slot] = bd[s, row_kind]

    def take_lines(s):
        @pl.when(at_col)
        def _():
            @pl.when(at_row)
            def _():
                many_lines(s, 0, N_PX - 1).wait_recv()

            @pl.when(jnp.logical_not(at_row))
            def _():
                many_lines(s, 0, N_PX).wait_recv()

            pair_copy(s, 0).start()
            many_lines(s, 1, N_PY - 1).wait_recv()
            pair_copy(s, 1).start()
            for cols in range(2):
                pair_copy(s, cols).wait_recv()

        @pl.when(at_row & jnp.logical_not(at_col))
        def _():
            many_lines(s, 0, 2 * N_PX - 1).wait_recv()
            many_lines(s, 1, 2 * N_PY).wait_recv()

    def make_ring(s):
        cells = jnp.concatenate([hal[s, slot] for slot in range(8)], axis=1)
        inner = dot(cells, sring[...])
        for q in range(3):
            for k in range(4):
                ring[4 * q + k] = inner[CB * q : CB * q + CB, 128 * k : 128 * k + 128]

        take_lines(s)

        @pl.when(border)
        def _():
            lane = iota((3 * CB, 128), 1)
            for side in range(2):
                parts = [linr[s, N_PX * side + j].astype(F32) for j in range(N_PX)]
                for k in range(4):
                    line = parts[0]
                    for j in range(1, N_PX):
                        line = jnp.where(lane // 32 == (k + j) % 4, parts[j], line)
                    if k:
                        line = pltpu.roll(line, 128 - 32 * k, 1)
                    line = line.astype(BF16)
                    for q in range(3):
                        full[12 * side + 4 * q + k] = line[CB * q : CB * q + CB, :]
            lane = iota((2 * CB, 128), 1)
            for last in range(2):
                parts = [
                    linc[s, N_PY * (j % 2) + (N_PY // 2) * last + j // 2].astype(F32)
                    for j in range(N_PY)
                ]
                for m in range(8):
                    line = parts[0]
                    for j in range(1, N_PY):
                        line = jnp.where(lane // 16 == (m + j) % 8, parts[j], line)
                    if m:
                        line = pltpu.roll(line, 128 - 16 * m, 1)
                    line = line.astype(BF16)
                    face = (m + 4 * last) % 8
                    full[12 * (2 + last) + face] = line[0:CB, :]
                    if face < 4:
                        full[12 * (2 + last) + 8 + face] = line[CB : 2 * CB, :]
            for edge in range(4):

                @pl.when(sides[edge])
                def _():
                    found = jnp.concatenate(
                        [full[12 * edge_ref[1, edge, f] + edge_ref[0, edge, f]] for f in range(FACES)],
                        axis=0,
                    )
                    both = dot(found, sedge[edge])
                    for f in range(FACES):
                        mine = both[CB * f : CB * f + CB]
                        ring[f] += jnp.where(
                            edge_ref[2, edge, f] == 1, mine[:, 128:256], mine[:, 0:128]
                        )

            for corner in range(4):

                @pl.when(sides[corner // 2] & sides[2 + corner % 2])
                def _():
                    found = jnp.concatenate(
                        [
                            full[12 * (corner_ref[corner, 1, f] // 2) + corner_ref[corner, 0, f]]
                            for f in range(FACES)
                        ],
                        axis=0,
                    )
                    both = dot(found, scorner[corner])
                    for f in range(FACES):
                        mine = both[CB * f : CB * f + CB]
                        ring[f] += jnp.where(
                            corner_ref[corner, 1, f] % 2 == 1, mine[:, 128:256], mine[:, 0:128]
                        )

        held[s, :, rows(ch), TILE:WIDE] = ring[...].astype(BF16)

    p = iota((CB, TILE), 1)
    a, b = p // RB, p % RB
    keep_a = (a >= 1, None, a < RA - 1)
    keep_b = (b >= 1, None, b < RB - 1)

    def inner_conv(s, part):
        for f in range(PARTS[part][0], sum(PARTS[part])):
            y = dot(wst[s], held[s, f, :, 0:TILE])
            total = None
            for dj in range(3):
                column = None
                for di in range(3):
                    tap = 3 * di + dj
                    term = y[CB * tap : CB * tap + CB]
                    if di != 1:
                        term = pltpu.roll(term, (-(di - 1) * RB) % TILE, 1)
                        term = jnp.where(keep_a[di], term, 0.0)
                    column = term if column is None else column + term
                if dj != 1:
                    column = pltpu.roll(column, (-(dj - 1)) % TILE, 1)
                    column = jnp.where(keep_b[dj], column, 0.0)
                total = column if total is None else total + column
            pre[f] = total

    def ring_conv(s):
        for f in range(FACES):
            y = dot(wst[s], held[s, f, :, TILE:WIDE])
            edge = jnp.concatenate([y[CB * tap : CB * tap + CB] for tap in range(9)], axis=1)
            high = edge.astype(BF16)
            ringy[f, 0:CB, :] = high
            ringy[f, CB : 2 * CB, :] = (edge - high.astype(F32)).astype(BF16)

        cells = ringy[...].reshape(2 * CB * FACES, 9 * RING)
        extra[...] = dot(cells, sconv[...]).reshape(FACES, 2, CB, TILE)

        def add_ring(g, carry):
            first = pl.multiple_of(4 * g, 4)
            more = extra[pl.ds(first, 4)]
            v = pre[pl.ds(first, 4)] + more[:, 0] + more[:, 1]
            if s == 0:
                sig = 1.0 / (1.0 + jnp.exp(-v))
                act_ref[pl.ds(first, 4)] = (v * sig).astype(BF16)
                slope = cot_ref[pl.ds(first, 4)].astype(F32) * sig * (1.0 + v * (1.0 - sig))
                held[1, pl.ds(first, 4), rows(ch), 0:TILE] = slope.astype(BF16)
            else:
                grad_ref[pl.ds(first, 4)] = v.astype(BF16)
            return carry

        lax.fori_loop(0, FACES // 4, add_ring, 0)

    for s in range(2):
        if s == 1:
            pack(1)
        send_lines(s)
        for n, (dx, dy, kind, slot) in enumerate(HALO):

            @pl.when(inside(px + dx, py + dy))
            def _():
                halo_copy(s, n).start()

        for index in (Z, XU, XD, Z + 1, Z + 2, Z + 3):
            ag_copy(s, index).start()

        def sent(*indices):
            for index in indices:
                ag_copy(s, index).wait_send()

        def came(*indices):
            for index in indices:
                ag_copy(s, index).wait_recv()

        def go(*indices):
            for index in indices:
                ag_copy(s, index).start()

        def ring_came(*indices):
            for index in indices:
                rg_copy(s, index).wait_recv()

        def ring_go(*indices):
            for index in indices:
                rg_copy(s, index).start()

        came(XU, XD)
        go(FU, FD)
        came(Z)
        go(ZU, ZD)
        came(Z + 1)
        go(ZU + 1, ZD + 1)
        for n, (dx, dy, kind, slot) in enumerate(HALO):

            @pl.when(inside(px - dx, py - dy))
            def _():
                halo_copy(s, n).wait_recv()

        make_ring(s)
        ring_go(0, 1, 2, 5)
        came(Z + 2)
        go(ZU + 2, ZD + 2, ZF + 2)
        came(ZU)
        go(ZF)
        came(ZD + 1)
        go(ZF + 1)
        came(Z + 3)
        go(ZU + 3, ZD + 3, ZF + 3)
        ring_came(0)
        ring_go(3, 4, 6)
        came(FU, FD, ZD, ZF)
        inner_conv(s, 0)
        came(ZU + 1, ZF + 1)
        inner_conv(s, 1)
        came(ZU + 2, ZD + 2, ZF + 2)
        inner_conv(s, 2)
        came(ZU + 3, ZD + 3, ZF + 3)
        inner_conv(s, 3)
        ring_came(1, 2, 3, 4, 5, 6)
        ring_conv(s)

    for s in range(2):
        for index in range(Z, ZF + 4):
            ag_copy(s, index).wait_send()
        for index in range(7):
            rg_copy(s, index).wait_send()
        for n, (dx, dy, kind, slot) in enumerate(HALO):

            @pl.when(inside(px + dx, py + dy))
            def _():
                halo_copy(s, n).wait_send()

        for cols in range(2):

            @pl.when((at_row, at_col)[cols])
            def _():
                many_lines(s, cols, FANOUT).wait_send()

            @pl.when(at_col)
            def _():
                pair_copy(s, cols).wait_send()


def local(features, cotangent, weight, edge_table, corner_table):
    def by_face(v):
        return jnp.transpose(v.reshape(CB, FACES, TILE), (1, 0, 2))

    smem = pl.BlockSpec(memory_space=pltpu.SMEM)
    hbm = pl.BlockSpec(memory_space=pl.ANY)
    field = pltpu.VMEM((FACES, CB, TILE), BF16)
    vmem = pl.BlockSpec(memory_space=pltpu.VMEM)
    act, grad = pl.pallas_call(
        kernel,
        out_shape=(field, field),
        in_specs=[smem, smem, hbm, hbm, hbm],
        out_specs=(vmem, vmem),
        scratch_shapes=[
            pltpu.VMEM((2, FACES, 8 * CB, WIDE), BF16),
            pltpu.VMEM((FACES, CB, TILE), BF16),
            pltpu.VMEM((9, 8 * CB, 8 * CB), BF16),
            pltpu.VMEM((2, 3, 3 * CB, 128), BF16),
            pltpu.VMEM((2, 2 * CB, 128), BF16),
            pltpu.VMEM((2, 8, 3 * CB, 128), BF16),
            pltpu.VMEM((2, FANOUT, 3 * CB, 128), BF16),
            pltpu.VMEM((2, 2 * N_PY, 2 * CB, 128), BF16),
            pltpu.VMEM((48, CB, 128), BF16),
            pltpu.VMEM((FACES, CB, RING), F32),
            pltpu.VMEM((FACES, CB, TILE), F32),
            pltpu.VMEM((FACES, 2 * CB, 9 * RING), BF16),
            pltpu.VMEM((FACES, 2, CB, TILE), F32),
            pltpu.VMEM((2, 9 * CB, 128), BF16),
            pltpu.VMEM((4, TILE, 128), BF16),
            pltpu.VMEM((1024, 512), BF16),
            pltpu.VMEM((4, 128, 256), BF16),
            pltpu.VMEM((4, 128, 256), BF16),
            pltpu.VMEM((9 * RING, TILE), BF16),
            pltpu.SemaphoreType.DMA((3,)),
            pltpu.SemaphoreType.DMA((2, ZF + 4)),
            pltpu.SemaphoreType.DMA((2, ZF + 4)),
            pltpu.SemaphoreType.DMA((2, 9)),
            pltpu.SemaphoreType.DMA((2, 9)),
            pltpu.SemaphoreType.DMA((2, 8)),
            pltpu.SemaphoreType.DMA((2, 8)),
            pltpu.SemaphoreType.DMA((2, 2)),
            pltpu.SemaphoreType.DMA((2, 2)),
            pltpu.SemaphoreType.DMA((2, 2)),
            pltpu.SemaphoreType.DMA((2, 2)),
        ],
        compiler_params=pltpu.CompilerParams(
            collective_id=0, has_side_effects=True, vmem_limit_bytes=56 * 1024 * 1024
        ),
        name="conv_pair",
    )(
        jnp.transpose(edge_table, (2, 1, 0)),
        jnp.transpose(corner_table, (1, 2, 0)),
        by_face(features),
        by_face(cotangent),
        weight.reshape(9, 8 * CB, 8 * CB),
    )

    def by_channel(v):
        return jnp.transpose(v, (1, 0, 2)).reshape(CB, FACES, 1, 1, TILE)

    return by_channel(act), by_channel(grad)


def solution(mesh):
    field = P("ch", None, "py", "px", None)
    return jax.shard_map(
        local,
        mesh=mesh,
        in_specs=(field, field, P(), P(), P()),
        out_specs=(field, field),
        check_vma=False,
    )
```
